256 devices in a mesh: seq: 16 (over x, y_hi, core), tensor: 16 (over y_lo, z).
Axes of the slice: x: 4, y: 4 (y_hi: 2, y_lo: 2; y = y_hi * 2 + y_lo), z: 8, core: 2. Of those that a mesh axis runs over, the one named last changes fastest.
Arguments:
- ssd_input: bfloat16 [6144, 8192], P('seq', 'tensor'), may hold values from -6 to 6
- gate_input: bfloat16 [6144, 8192], P('seq', 'tensor'), may hold values from -6 to 6
- state_maps: bfloat16 [6144, 2, 2048], P('seq', None, 'tensor'), may hold values from -2 to 2
- step_raw: float32 [6144, 64], P('seq', 'tensor'), may hold values from -3 to 3
- step_bias: float32 [64], P('tensor'), may hold values from -1 to 0
- decay_rate: float32 [64], P('tensor'), may hold values from 0.00043402778 to 0.1, as said below
- skip_gain: float32 [64], P('tensor'), may hold values from 0.5 to 1.5
- norm_gain: float32 [8192], P('tensor'), may hold values from 0.1 to 1.9
- out_weight: bfloat16 [4096, 8192], P(None, 'tensor'), may hold values from -0.176776695 to 0.176776695
- reward_head: float32 [4096], replicated, may hold values from -0.25 to 0.25
- traj_lengths: int32 [32], replicated, may hold values from 1 to 1152, 6144 in all
- step_pairs: int32 [6144], replicated, may hold values from 0 to 6143, each once
Outputs:
- rewards: float32 [6144], P('seq')
- grad_input: bfloat16 [6144, 8192], P('seq', 'tensor')
- grad_gate: bfloat16 [6144, 8192], P('seq', 'tensor')
- grad_maps: bfloat16 [6144, 2, 2048], P('seq', None, 'tensor')
- grad_step: float32 [6144, 64], P('seq', 'tensor')
The draws below stay inside these ranges and needn't reach their ends.
Inputs may be any that keep to these rules, and one draw needn't show every extreme that they name: `traj_lengths`: trajectory lengths sum to 6144; the longest is exactly 1152. A permutation of the token positions; step_pairs[2k] is the chosen and step_pairs[2k+1] the rejected step of pair k. `decay_rate`: positive decay rates.
All inputs are finite; a program needn't handle non-finite values.
Results may differ from the reference program's by a relative error of at most 0.006.
Values may be sent and summed in bfloat16 or wider, within the bound.
A program may use at most 64 MiB of HBM per device.

```python
import math
import jax
import jax.numpy as jnp
import numpy as np
from jax import lax

D = 4096
HEADS = 64
HEAD_DIM = 128
STATE = 128
GROUPS = 16
TOK_DEV = 384
TOKENS = 6144
MAXTRAJ = 1152
NTRAJ = 32
N_SEQ = 16
N_TENSOR = 16


def rising(count, factor):
    return jnp.power(factor, jnp.arange(count, dtype=jnp.float32) / (count - 1))


def draw_decay_rate(key, part):
    low_end = math.log(1.0 / (2.0 * TOK_DEV))
    high_end = math.log(0.1)
    uniform_part = jax.random.uniform(key, (HEADS,), jnp.float32)
    return jnp.exp(low_end + (high_end - low_end) * uniform_part)


def draw_out_weight(key, part):
    fan_in = HEADS * HEAD_DIM
    base_draw = jnp.clip(jax.random.normal(key, (D, fan_in), jnp.float32), -4.0, 4.0)
    row_lift = rising(D, 3.0)
    return (base_draw * row_lift[:, None] * fan_in ** (-0.5)).astype(jnp.bfloat16)


def draw_reward_head(key, part):
    base_draw = jnp.clip(jax.random.normal(key, (D,), jnp.float32), -4.0, 4.0)
    row_lift = rising(D, 3.0)
    return base_draw * row_lift * D ** (-0.5)


def steps_of(stream_key, dims, pieces, low, top_value):
    loudness = 1.0
    for axis_at, parts in pieces:
        steps = jax.random.uniform(jax.random.fold_in(jax.random.fold_in(stream_key, 6), axis_at), (parts,), jnp.float32, low / len(pieces), top_value / len(pieces))
        loudness = loudness * jnp.repeat(jnp.exp(steps), dims[axis_at] // parts).reshape((-1,) + (1,) * (len(dims) - 1 - axis_at))
    return loudness


def split_up(number_of, total, reach, slope):
    weights = [(1 << 20) // math.isqrt(standing ** slope) + 1 for standing in range(2, number_of + 1)]
    rest, holding = total - reach - (number_of - 1), [1] * (number_of - 1)
    while rest > 0:
        movable = [i for i in range(number_of - 1) if holding[i] < reach]
        whole, remaining = sum([weights[i] for i in movable]), rest
        for i in movable:
            addition = min(reach - holding[i], max(1, remaining * weights[i] // whole), rest)
            holding[i] = holding[i] + addition
            rest = rest - addition
    return np.array([reach] + holding)


def uneven_parts(key, amount, total, reach, skew):
    if amount == 2:
        one = jax.random.randint(key, (), max(1, total - reach), min(reach, total - 1) + 1)
        return jnp.stack([one, total - one])
    tallies = jnp.asarray(split_up(amount, total, reach, skew), jnp.int32)
    couples = (amount - 1) // 2
    donor, sink = tallies[1:1 + 2 * couples:2], tallies[2:2 + 2 * couples:2]
    margin = jnp.minimum(donor - 1, reach - sink)
    shifted = jax.random.randint(jax.random.fold_in(key, 1), (couples,), 0, 1 << 20) % (margin + 1)
    tallies = tallies.at[1:1 + 2 * couples:2].set(donor - shifted).at[2:2 + 2 * couples:2].set(sink + shifted)
    return tallies[jax.random.permutation(jax.random.fold_in(key, 2), amount)]


def bell_draw(key, shape, deviation, bound, shards=(), kind=jnp.bfloat16):
    loudness = steps_of(key, shape, shards, -0.22, 0.18) if shards else 1.0
    values = jax.random.normal(key, shape, jnp.float32) * deviation * loudness
    return jnp.minimum(jnp.maximum(values, -bound), bound).astype(kind)


def setup_inputs(seed: int = 0) -> dict:
    splits = jax.random.split(jax.random.key(seed), 13)
    return {
        "ssd_input": bell_draw(splits[0], (TOKENS, HEADS * HEAD_DIM), 1.0, 6.0, ((0, 16), (1, 16))),
        "gate_input": bell_draw(splits[1], (TOKENS, HEADS * HEAD_DIM), 1.0, 6.0, ((0, 16), (1, 16))),
        "state_maps": bell_draw(splits[2], (TOKENS, 2, GROUPS * STATE), 0.3, 2.0, ((0, 16), (2, 16))),
        "step_raw": bell_draw(splits[3], (TOKENS, HEADS), 0.5, 3.0, ((0, 16), (1, 16)), jnp.float32),
        "step_bias": jnp.clip(-1.0 + 1.0 * jax.random.uniform(splits[4], (HEADS,), jnp.float32) ** steps_of(splits[4], (HEADS,), ((0, 16),), -0.2, 0.2), -1.0, 0.0),
        "decay_rate": draw_decay_rate(jax.random.fold_in(splits[12], 71), 0),
        "skip_gain": jnp.clip(0.5 + 1.0 * jax.random.uniform(splits[6], (HEADS,), jnp.float32) ** steps_of(splits[6], (HEADS,), ((0, 16),), -0.2, 0.2), 0.5, 1.5),
        "norm_gain": jnp.clip(1.0 + 0.18 * jax.random.normal(splits[7], (HEADS * HEAD_DIM,), jnp.float32), 0.1, 1.9),
        "out_weight": draw_out_weight(jax.random.fold_in(splits[12], 71), 0),
        "reward_head": draw_reward_head(jax.random.fold_in(splits[12], 71), 0),
        "traj_lengths": uneven_parts(splits[10], NTRAJ, TOKENS, MAXTRAJ, 2).astype(jnp.int32),
        "step_pairs": jax.random.permutation(splits[11], TOKENS).astype(jnp.int32),
    }


norm_eps = 1e-05
loss_scale = 64.0
highest = lax.Precision.HIGHEST

def prepare(step_raw, step_bias, decay_rate, starts):
    step_size = jax.nn.softplus(step_raw + step_bias[None, :])
    cumulative = jnp.cumsum(-step_size * decay_rate[None, :], axis=0)
    segment = jnp.cumsum(starts)
    return (step_size, cumulative, segment)

def local_out(x_heads, z_heads, b_rows, c_rows, step_raw, state_in, step_bias, decay_rate, skip_gain, norm_gain, starts):
    row_count, head_count, head_width = x_heads.shape
    group_count = b_rows.shape[1]
    per_group = head_count // group_count
    step_size, cumulative, segment = prepare(step_raw, step_bias, decay_rate, starts)
    earlier = jnp.arange(row_count)[None, :] <= jnp.arange(row_count)[:, None]
    same_segment = segment[:, None] == segment[None, :]
    allowed = (earlier & same_segment)[:, :, None]
    spread = cumulative[:, None, :] - cumulative[None, :, :]
    decay_matrix = jnp.where(allowed, jnp.exp(jnp.where(allowed, spread, 0.0)), 0.0)
    scores = jnp.einsum('tgn,sgn->tsg', c_rows, b_rows, precision=highest)
    mixing = decay_matrix.reshape(row_count, row_count, group_count, per_group) * scores[:, :, :, None] * step_size.reshape(1, row_count, group_count, per_group)
    grouped_x = x_heads.reshape(row_count, group_count, per_group, head_width)
    within_part = jnp.einsum('tsgh,sghp->tghp', mixing, grouped_x, precision=highest)
    carried = jnp.einsum('tgn,ghnp->tghp', c_rows, state_in.reshape(group_count, per_group, -1, head_width), precision=highest)
    first_weight = jnp.where(segment[:, None] == 0, jnp.exp(cumulative), 0.0)
    carried_part = carried * first_weight.reshape(row_count, group_count, per_group, 1)
    mixed_heads = within_part + carried_part + skip_gain.reshape(1, group_count, per_group, 1) * grouped_x
    gated_heads = mixed_heads * jax.nn.silu(z_heads.reshape(row_count, group_count, per_group, head_width))
    mean_square = lax.optimization_barrier(jnp.mean(gated_heads * gated_heads, axis=(2, 3), keepdims=True))
    normed = gated_heads * lax.rsqrt(mean_square + norm_eps) * norm_gain.reshape(1, group_count, per_group, head_width)
    return normed.reshape(row_count, head_count * head_width)

def local_state(x_heads, b_rows, step_raw, step_bias, decay_rate, starts):
    row_count, head_count, head_width = x_heads.shape
    group_count = b_rows.shape[1]
    per_group = head_count // group_count
    step_size, cumulative, segment = prepare(step_raw, step_bias, decay_rate, starts)
    last_segment = segment[-1]
    weight = jnp.where((segment == last_segment)[:, None], jnp.exp(cumulative[-1][None, :] - cumulative), 0.0) * step_size
    state_sum = jnp.einsum('sgn,sgh,sghp->ghnp', b_rows, weight.reshape(row_count, group_count, per_group), x_heads.reshape(row_count, group_count, per_group, head_width), precision=highest)
    through = jnp.where(last_segment == 0, jnp.exp(cumulative[-1]), 0.0)
    return (state_sum.reshape(head_count, -1, head_width), through)

def reference(ssd_input, gate_input, state_maps, step_raw, step_bias, decay_rate, skip_gain, norm_gain, out_weight, reward_head, traj_lengths, step_pairs):
    row_count = TOK_DEV
    head_count = HEADS // N_TENSOR
    group_count = GROUPS // N_TENSOR
    head_width = HEAD_DIM
    channel_count = head_count * head_width
    positions = jnp.arange(TOKENS, dtype=jnp.int32)
    openings = jnp.cumsum(traj_lengths) - traj_lengths
    starts = jnp.any(positions[:, None] == openings[None, :], axis=1).astype(jnp.float32)
    start_blocks = starts.reshape(N_SEQ, row_count)
    group_ids = jnp.arange(N_TENSOR, dtype=jnp.int32)

    def slices(group_index):
        x_blocks = lax.dynamic_slice_in_dim(ssd_input, group_index * channel_count, channel_count, 1).astype(jnp.float32).reshape(N_SEQ, row_count, head_count, head_width)
        z_blocks = lax.dynamic_slice_in_dim(gate_input, group_index * channel_count, channel_count, 1).astype(jnp.float32).reshape(N_SEQ, row_count, head_count, head_width)
        b_blocks = lax.dynamic_slice_in_dim(state_maps[:, 0], group_index * (group_count * STATE), group_count * STATE, 1).astype(jnp.float32).reshape(N_SEQ, row_count, group_count, STATE)
        c_blocks = lax.dynamic_slice_in_dim(state_maps[:, 1], group_index * (group_count * STATE), group_count * STATE, 1).astype(jnp.float32).reshape(N_SEQ, row_count, group_count, STATE)
        step_blocks = lax.dynamic_slice_in_dim(step_raw, group_index * head_count, head_count, 1).reshape(N_SEQ, row_count, head_count)
        bias_part = lax.dynamic_slice_in_dim(step_bias, group_index * head_count, head_count, 0)
        rate_part = lax.dynamic_slice_in_dim(decay_rate, group_index * head_count, head_count, 0)
        skip_part = lax.dynamic_slice_in_dim(skip_gain, group_index * head_count, head_count, 0)
        gain_part = lax.dynamic_slice_in_dim(norm_gain, group_index * channel_count, channel_count, 0)
        return (x_blocks, z_blocks, b_blocks, c_blocks, step_blocks, bias_part, rate_part, skip_part, gain_part)
    zero_state = jnp.zeros((head_count, STATE, head_width), jnp.float32)

    def forward_group(group_index):
        x_blocks, z_blocks, b_blocks, c_blocks, step_blocks, bias_part, rate_part, skip_part, gain_part = slices(group_index)

        def block_step(state_in, block_data):
            x_heads, z_heads, b_rows, c_rows, step_rows, start_rows = block_data
            normed = local_out(x_heads, z_heads, b_rows, c_rows, step_rows, state_in, bias_part, rate_part, skip_part, gain_part, start_rows)
            state_sum, through = local_state(x_heads, b_rows, step_rows, bias_part, rate_part, start_rows)
            return (through[:, None, None] * state_in + state_sum, normed.astype(jnp.bfloat16))
        _, mixed_blocks = lax.scan(block_step, zero_state, (x_blocks, z_blocks, b_blocks, c_blocks, step_blocks, start_blocks))
        return mixed_blocks.reshape(TOKENS, channel_count)
    mixed_groups = lax.map(forward_group, group_ids)
    mixed_all = jnp.moveaxis(mixed_groups, 0, 1).reshape(TOKENS, HEADS * HEAD_DIM)
    hidden = lax.dot_general(out_weight, mixed_all, (((1,), (1,)), ((), ())), preferred_element_type=jnp.float32)
    squares = lax.optimization_barrier(jnp.sum(hidden * hidden, axis=0))
    along = lax.optimization_barrier(jnp.sum(hidden * reward_head[:, None], axis=0))
    scale = jnp.sqrt(squares / D + norm_eps)
    rewards = along / scale
    chosen = step_pairs[0::2]
    rejected = step_pairs[1::2]
    pair_push = loss_scale * jax.nn.sigmoid(rewards[rejected] - rewards[chosen])
    pair_grad = jnp.zeros((TOKENS,), jnp.float32).at[chosen].add(-pair_push).at[rejected].add(pair_push)
    d_hidden = (pair_grad[None, :] * (reward_head[:, None] / scale[None, :] - along[None, :] * hidden / (D * scale * scale * scale)[None, :])).astype(jnp.bfloat16)
    d_mixed = lax.dot_general(d_hidden, out_weight, (((0,), (0,)), ((), ())), preferred_element_type=jnp.float32)

    def backward_group(group_index):
        x_blocks, z_blocks, b_blocks, c_blocks, step_blocks, bias_part, rate_part, skip_part, gain_part = slices(group_index)
        mixed_grads = lax.dynamic_slice_in_dim(d_mixed, group_index * channel_count, channel_count, 1).reshape(N_SEQ, row_count, channel_count)

        def first_pass(state_in, block_data):
            x_heads, z_heads, b_rows, c_rows, step_rows, start_rows, grad_rows = block_data

            def out_part(a_in, b_in, c_in, d_in, e_in, f_in):
                return local_out(a_in, b_in, c_in, d_in, e_in, f_in, bias_part, rate_part, skip_part, gain_part, start_rows)
            _, pull_back = jax.vjp(out_part, x_heads, z_heads, b_rows, c_rows, step_rows, state_in)
            gradients = pull_back(grad_rows)
            state_sum, through = local_state(x_heads, b_rows, step_rows, bias_part, rate_part, start_rows)
            return (through[:, None, None] * state_in + state_sum, (gradients, through, state_in))
        _, (first_grads, throughs, states_in) = lax.scan(first_pass, zero_state, (x_blocks, z_blocks, b_blocks, c_blocks, step_blocks, start_blocks, mixed_grads))

        def second_pass(grad_end, block_data):
            x_heads, b_rows, step_rows, start_rows, grad_in, through, state_in = block_data

            def state_part(a_in, b_in, c_in):
                return local_state(a_in, b_in, c_in, bias_part, rate_part, start_rows)
            _, pull_back = jax.vjp(state_part, x_heads, b_rows, step_rows)
            gradients = pull_back((grad_end, lax.optimization_barrier(jnp.sum(grad_end * state_in, axis=(1, 2)))))
            return (grad_in + through[:, None, None] * grad_end, gradients)
        _, second_grads = lax.scan(second_pass, zero_state, (x_blocks, b_blocks, step_blocks, start_blocks, first_grads[5], throughs, states_in), reverse=True)
        grad_x = (first_grads[0] + second_grads[0]).reshape(TOKENS, channel_count).astype(jnp.bfloat16)
        grad_z = first_grads[1].reshape(TOKENS, channel_count).astype(jnp.bfloat16)
        grad_b = (first_grads[2] + second_grads[1]).reshape(TOKENS, group_count * STATE)
        grad_c = first_grads[3].reshape(TOKENS, group_count * STATE)
        grad_maps = jnp.stack([grad_b, grad_c], axis=1).astype(jnp.bfloat16)
        grad_dt = (first_grads[4] + second_grads[2]).reshape(TOKENS, head_count)
        return (grad_x, grad_z, grad_maps, grad_dt)
    results = lax.map(backward_group, group_ids)
    grad_input = jnp.moveaxis(results[0], 0, 1).reshape(TOKENS, HEADS * HEAD_DIM)
    grad_gate = jnp.moveaxis(results[1], 0, 1).reshape(TOKENS, HEADS * HEAD_DIM)
    grad_maps = jnp.moveaxis(results[2], 0, 2).reshape(TOKENS, 2, GROUPS * STATE)
    grad_step = jnp.moveaxis(results[3], 0, 1).reshape(TOKENS, HEADS)
    return (rewards, grad_input, grad_gate, grad_maps, grad_step)
```

```python
import jax
import jax.numpy as jnp
from jax import lax
from jax.sharding import PartitionSpec as P

STATE = 128


norm_eps = 1e-05
loss_scale = 64.0
longest = 1152
highest = lax.Precision.HIGHEST


def shifted(value, axis, distance):
    size = lax.axis_size(axis)
    return jax.tree.map(
        lambda part: lax.ppermute(part, axis, [(i, (i + distance) % size) for i in range(size)]),
        value,
    )


def neighbours(through, state, axis, step, reach):
    total, carry = None, None
    for k in range(1, reach + 1):
        far_through, far_state = shifted((through, state.astype(jnp.bfloat16)), axis, k * step)
        far_state = far_state.astype(jnp.float32)
        if total is None:
            total, carry = far_state, far_through
        else:
            total = total + carry[:, None, None] * far_state
            carry = carry * far_through
    return total


def prepare(step_raw, step_bias, decay_rate, starts):
    step_size = jax.nn.softplus(step_raw + step_bias[None, :])
    cumulative = jnp.cumsum(-step_size * decay_rate[None, :], axis=0)
    segment = jnp.cumsum(starts)
    return (step_size, cumulative, segment)


def local_out(
    x_heads,
    z_heads,
    b_rows,
    c_rows,
    step_raw,
    state_in,
    step_bias,
    decay_rate,
    skip_gain,
    norm_gain,
    starts,
):
    row_count, head_count, head_width = x_heads.shape
    group_count = b_rows.shape[1]
    per_group = head_count // group_count
    step_size, cumulative, segment = prepare(step_raw, step_bias, decay_rate, starts)
    earlier = jnp.arange(row_count)[None, :] <= jnp.arange(row_count)[:, None]
    same_segment = segment[:, None] == segment[None, :]
    allowed = (earlier & same_segment)[:, :, None]
    spread = cumulative[:, None, :] - cumulative[None, :, :]
    decay_matrix = jnp.where(allowed, jnp.exp(jnp.where(allowed, spread, 0.0)), 0.0)
    scores = jnp.einsum("tgn,sgn->tsg", c_rows, b_rows, precision=highest)
    mixing = (
        decay_matrix.reshape(row_count, row_count, group_count, per_group)
        * scores[:, :, :, None]
        * step_size.reshape(1, row_count, group_count, per_group)
    )
    grouped_x = x_heads.reshape(row_count, group_count, per_group, head_width)
    within_part = jnp.einsum("tsgh,sghp->tghp", mixing, grouped_x, precision=highest)
    carried = jnp.einsum(
        "tgn,ghnp->tghp",
        c_rows,
        state_in.reshape(group_count, per_group, -1, head_width),
        precision=highest,
    )
    first_weight = jnp.where(segment[:, None] == 0, jnp.exp(cumulative), 0.0)
    carried_part = carried * first_weight.reshape(row_count, group_count, per_group, 1)
    mixed_heads = (
        within_part + carried_part + skip_gain.reshape(1, group_count, per_group, 1) * grouped_x
    )
    gated_heads = mixed_heads * jax.nn.silu(
        z_heads.reshape(row_count, group_count, per_group, head_width)
    )
    mean_square = jnp.mean(gated_heads * gated_heads, axis=(2, 3), keepdims=True)
    normed = (
        gated_heads
        * lax.rsqrt(mean_square + norm_eps)
        * norm_gain.reshape(1, group_count, per_group, head_width)
    )
    return normed.reshape(row_count, head_count * head_width)


def local_state(x_heads, b_rows, step_raw, step_bias, decay_rate, starts):
    row_count, head_count, head_width = x_heads.shape
    group_count = b_rows.shape[1]
    per_group = head_count // group_count
    step_size, cumulative, segment = prepare(step_raw, step_bias, decay_rate, starts)
    last_segment = segment[-1]
    weight = (
        jnp.where(
            (segment == last_segment)[:, None], jnp.exp(cumulative[-1][None, :] - cumulative), 0.0
        )
        * step_size
    )
    state_sum = jnp.einsum(
        "sgn,sgh,sghp->ghnp",
        b_rows,
        weight.reshape(row_count, group_count, per_group),
        x_heads.reshape(row_count, group_count, per_group, head_width),
        precision=highest,
    )
    through = jnp.where(last_segment == 0, jnp.exp(cumulative[-1]), 0.0)
    return (state_sum.reshape(head_count, -1, head_width), through)


def on_device(
    ssd_input,
    gate_input,
    state_maps,
    step_raw,
    step_bias,
    decay_rate,
    skip_gain,
    norm_gain,
    out_weight,
    reward_head,
    traj_lengths,
    step_pairs,
):
    row_count = ssd_input.shape[0]
    head_count = step_raw.shape[1]
    head_width = ssd_input.shape[1] // head_count
    group_count = state_maps.shape[2] // STATE
    model_width = out_weight.shape[0]
    offset = lax.axis_index("seq") * row_count
    positions = offset + jnp.arange(row_count, dtype=jnp.int32)
    openings = jnp.cumsum(traj_lengths) - traj_lengths
    starts = jnp.any(positions[:, None] == openings[None, :], axis=1).astype(jnp.float32)
    x_heads = ssd_input.astype(jnp.float32).reshape(row_count, head_count, head_width)
    z_heads = gate_input.astype(jnp.float32).reshape(row_count, head_count, head_width)
    b_rows = state_maps[:, 0].astype(jnp.float32).reshape(row_count, group_count, STATE)
    c_rows = state_maps[:, 1].astype(jnp.float32).reshape(row_count, group_count, STATE)

    def state_part(a_in, b_in, c_in):
        return local_state(a_in, b_in, c_in, step_bias, decay_rate, starts)

    (state_local, through), pull_state = jax.vjp(state_part, x_heads, b_rows, step_raw)
    reach = -(-(longest - 1) // row_count)
    state_in = neighbours(through, state_local, "seq", 1, reach)

    def out_part(a_in, b_in, c_in, d_in, e_in, f_in):
        return local_out(
            a_in, b_in, c_in, d_in, e_in, f_in, step_bias, decay_rate, skip_gain, norm_gain, starts
        )

    normed, pull_out = jax.vjp(out_part, x_heads, z_heads, b_rows, c_rows, step_raw, state_in)
    mixed = normed.astype(jnp.bfloat16)
    hidden_part = lax.dot_general(
        out_weight, mixed, (((1,), (1,)), ((), ())), preferred_element_type=jnp.float32
    ).astype(jnp.bfloat16)
    hidden = lax.psum_scatter(hidden_part, "tensor", scatter_dimension=0, tiled=True)
    reward_channels = jnp.sum(out_weight.astype(jnp.float32) * reward_head[:, None], axis=0)
    hidden_f = hidden.astype(jnp.float32)
    along_part = jnp.sum(mixed.astype(jnp.float32) * reward_channels[None, :], axis=1)
    squares_part = jnp.sum(hidden_f * hidden_f, axis=0)
    own_along, own_squares = lax.psum(jnp.stack([along_part, squares_part]), "tensor")
    own_scale = jnp.sqrt(own_squares / model_width + norm_eps)
    own_rewards = own_along / own_scale
    rewards_all = lax.all_gather(own_rewards, "seq", axis=0, tiled=True)
    hidden_all = lax.all_gather(hidden, "tensor", axis=0, tiled=True)
    pair_rows = step_pairs.reshape(-1, 2)
    mates = pair_rows[:, ::-1].reshape(1, -1)
    signs = jnp.where(jnp.arange(step_pairs.shape[0]) % 2 == 0, -1.0, 1.0)[None, :]
    hit = positions[:, None] == step_pairs[None, :]
    mate = jnp.sum(jnp.where(hit, mates, 0), axis=1)
    sign = jnp.sum(jnp.where(hit, signs, 0.0), axis=1)
    all_tokens = jnp.arange(step_pairs.shape[0], dtype=jnp.int32)
    mate_reward = jnp.sum(
        jnp.where(mate[:, None] == all_tokens[None, :], rewards_all[None, :], 0.0), axis=1
    )
    own_grad = sign * loss_scale * jax.nn.sigmoid(sign * (own_rewards - mate_reward))
    hidden_back = lax.dot_general(
        hidden_all, out_weight, (((0,), (0,)), ((), ())), preferred_element_type=jnp.float32
    )
    d_mixed = (own_grad / own_scale)[:, None] * (
        reward_channels[None, :]
        - (own_along / (model_width * own_scale * own_scale))[:, None] * hidden_back
    )
    out_grads = pull_out(d_mixed)
    grad_in = out_grads[5]
    grad_end = neighbours(through, grad_in, "seq", -1, reach)
    state_grads = pull_state((grad_end, jnp.sum(grad_end * state_in, axis=(1, 2))))
    grad_input = (
        (out_grads[0] + state_grads[0])
        .reshape(row_count, head_count * head_width)
        .astype(jnp.bfloat16)
    )
    grad_gate = out_grads[1].reshape(row_count, head_count * head_width).astype(jnp.bfloat16)
    grad_b = (out_grads[2] + state_grads[1]).reshape(row_count, group_count * STATE)
    grad_c = out_grads[3].reshape(row_count, group_count * STATE)
    grad_maps = jnp.stack([grad_b, grad_c], axis=1).astype(jnp.bfloat16)
    grad_step = out_grads[4] + state_grads[2]
    return (own_rewards, grad_input, grad_gate, grad_maps, grad_step)


def solution(mesh):
    return jax.shard_map(
        on_device,
        mesh=mesh,
        in_specs=(
            P("seq", "tensor"),
            P("seq", "tensor"),
            P("seq", None, "tensor"),
            P("seq", "tensor"),
            P("tensor"),
            P("tensor"),
            P("tensor"),
            P("tensor"),
            P(None, "tensor"),
            P(),
            P(),
            P(),
        ),
        out_specs=(
            P("seq"),
            P("seq", "tensor"),
            P("seq", "tensor"),
            P("seq", None, "tensor"),
            P("seq", "tensor"),
        ),
        check_vma=False,
    )
```

```python
import jax
import jax.numpy as jnp
from jax import lax
from jax.experimental import pallas as pl
from jax.experimental.pallas import tpu as pltpu
from jax.sharding import PartitionSpec as P

STATE = 128


norm_eps = 1e-05
loss_scale = 64.0
longest = 1152
MESH = pl.DeviceIdType.MESH
highest = lax.Precision.HIGHEST


def shifted(value, axis, distance):
    size = lax.axis_size(axis)
    return jax.tree.map(
        lambda part: lax.ppermute(part, axis, [(i, (i + distance) % size) for i in range(size)]),
        value,
    )


def neighbours(through, state, axis, step, reach):
    total, carry = None, None
    for k in range(1, reach + 1):
        far_through, far_state = shifted((through, state.astype(jnp.bfloat16)), axis, k * step)
        far_state = far_state.astype(jnp.float32)
        if total is None:
            total, carry = far_state, far_through
        else:
            total = total + carry[:, None, None] * far_state
            carry = carry * far_through
    return total


def prepare(step_raw, step_bias, decay_rate, starts):
    step_size = jax.nn.softplus(step_raw + step_bias[None, :])
    cumulative = jnp.cumsum(-step_size * decay_rate[None, :], axis=0)
    segment = jnp.cumsum(starts)
    return (step_size, cumulative, segment)


def local_out(
    x_heads,
    z_heads,
    b_rows,
    c_rows,
    step_raw,
    state_in,
    step_bias,
    decay_rate,
    skip_gain,
    norm_gain,
    starts,
):
    row_count, head_count, head_width = x_heads.shape
    group_count = b_rows.shape[1]
    per_group = head_count // group_count
    step_size, cumulative, segment = prepare(step_raw, step_bias, decay_rate, starts)
    earlier = jnp.arange(row_count)[None, :] <= jnp.arange(row_count)[:, None]
    same_segment = segment[:, None] == segment[None, :]
    allowed = (earlier & same_segment)[:, :, None]
    spread = cumulative[:, None, :] - cumulative[None, :, :]
    decay_matrix = jnp.where(allowed, jnp.exp(jnp.where(allowed, spread, 0.0)), 0.0)
    scores = jnp.einsum("tgn,sgn->tsg", c_rows, b_rows, precision=highest)
    mixing = (
        decay_matrix.reshape(row_count, row_count, group_count, per_group)
        * scores[:, :, :, None]
        * step_size.reshape(1, row_count, group_count, per_group)
    )
    grouped_x = x_heads.reshape(row_count, group_count, per_group, head_width)
    within_part = jnp.einsum("tsgh,sghp->tghp", mixing, grouped_x, precision=highest)
    carried = jnp.einsum(
        "tgn,ghnp->tghp",
        c_rows,
        state_in.reshape(group_count, per_group, -1, head_width),
        precision=highest,
    )
    first_weight = jnp.where(segment[:, None] == 0, jnp.exp(cumulative), 0.0)
    carried_part = carried * first_weight.reshape(row_count, group_count, per_group, 1)
    mixed_heads = (
        within_part + carried_part + skip_gain.reshape(1, group_count, per_group, 1) * grouped_x
    )
    gated_heads = mixed_heads * jax.nn.silu(
        z_heads.reshape(row_count, group_count, per_group, head_width)
    )
    mean_square = jnp.mean(gated_heads * gated_heads, axis=(2, 3), keepdims=True)
    normed = (
        gated_heads
        * lax.rsqrt(mean_square + norm_eps)
        * norm_gain.reshape(1, group_count, per_group, head_width)
    )
    return normed.reshape(row_count, head_count * head_width)


def local_state(x_heads, b_rows, step_raw, step_bias, decay_rate, starts):
    row_count, head_count, head_width = x_heads.shape
    group_count = b_rows.shape[1]
    per_group = head_count // group_count
    step_size, cumulative, segment = prepare(step_raw, step_bias, decay_rate, starts)
    last_segment = segment[-1]
    weight = (
        jnp.where(
            (segment == last_segment)[:, None], jnp.exp(cumulative[-1][None, :] - cumulative), 0.0
        )
        * step_size
    )
    state_sum = jnp.einsum(
        "sgn,sgh,sghp->ghnp",
        b_rows,
        weight.reshape(row_count, group_count, per_group),
        x_heads.reshape(row_count, group_count, per_group, head_width),
        precision=highest,
    )
    through = jnp.where(last_segment == 0, jnp.exp(cumulative[-1]), 0.0)
    return (state_sum.reshape(head_count, -1, head_width), through)


def exchange_kernel(
    mixed_ref,
    weight_ref,
    channel_ref,
    back_ref,
    stats_ref,
    rewards_ref,
    first,
    moving,
    swap_out,
    swap_in,
    hidden,
    own_stats,
    far_stats,
    own_reward,
    reduce_send,
    reduce_recv,
    swap_send,
    swap_recv,
    gather_send,
    gather_recv,
    stats_send,
    stats_recv,
    reward_send,
    reward_recv,
):
    seq, tensor = lax.axis_index("seq"), lax.axis_index("tensor")
    seq_count, tensor_count = lax.axis_size("seq"), lax.axis_size("tensor")
    chips = tensor_count // 2
    place, side = lax.rem(tensor, chips), tensor // chips
    base = side * chips
    up = (seq, base + lax.rem(place + 1, chips))
    down = (seq, base + lax.rem(place + chips - 1, chips))
    across = (seq, (1 - side) * chips + place)
    ways = (up, down)
    tokens = mixed_ref.shape[0]
    model_width = weight_ref.shape[0]
    half = hidden.shape[-1]
    pieces = hidden.shape[2]
    piece = tokens // pieces

    barrier = pltpu.get_barrier_semaphore()

    def greet_tensor(k, _):
        other = lax.rem(tensor + k, tensor_count)
        pl.semaphore_signal(barrier, inc=1, device_id=(seq, other), device_id_type=MESH)
        return 0

    def greet_seq(k, _):
        other = lax.rem(seq + k, seq_count)
        pl.semaphore_signal(barrier, inc=1, device_id=(other, tensor), device_id_type=MESH)
        return 0

    lax.fori_loop(1, tensor_count, greet_tensor, 0)
    lax.fori_loop(1, seq_count, greet_seq, 0)

    def chunk(way, distance):
        move = distance if way == 1 else chips - distance
        return lax.rem(place + move, chips)

    def rows(index, way):
        return pl.ds(pl.multiple_of((index * 2 + way) * half, half), half)

    def own_part(way, distance):
        return lax.dot_general(
            mixed_ref[...],
            weight_ref[rows(chunk(way, distance), way), :],
            (((1,), (1,)), ((), ())),
            preferred_element_type=jnp.float32,
        )

    def reduce_copy(way, step, j, source):
        return pltpu.make_async_remote_copy(
            src_ref=source,
            dst_ref=moving.at[way, step, j],
            send_sem=reduce_send.at[way, step, j],
            recv_sem=reduce_recv.at[way, step, j],
            device_id=ways[way],
            device_id_type=MESH,
        )

    def reduce_source(way, step, j):
        return first.at[way, j] if step is None else moving.at[way, step, j]

    for way in range(2):
        part = own_part(way, 1)
        for j in range(pieces):
            first[way, j] = part[j * piece : (j + 1) * piece].astype(jnp.bfloat16)
    pl.semaphore_wait(barrier, tensor_count + seq_count - 2)
    for j in range(pieces):
        for way in range(2):
            reduce_copy(way, 0, j, first.at[way, j]).start()

    along = lax.dot_general(
        jnp.broadcast_to(channel_ref[...], (8, channel_ref.shape[1])),
        mixed_ref[...].astype(jnp.float32),
        (((1,), (1,)), ((), ())),
        preferred_element_type=jnp.float32,
        precision=lax.Precision.HIGHEST,
    )

    def reduce_step(step, _):
        parts = [own_part(way, step + 2) for way in range(2)]
        for j in range(pieces):
            for way in range(2):
                reduce_copy(way, step, j, moving.at[way, step, j]).wait_recv()
                moving[way, step, j] = (
                    moving[way, step, j].astype(jnp.float32)
                    + parts[way][j * piece : (j + 1) * piece]
                ).astype(jnp.bfloat16)
                reduce_copy(way, step + 1, j, moving.at[way, step, j]).start()
        return 0

    lax.fori_loop(0, chips - 2, reduce_step, 0)

    def swap_copy(way, j):
        return pltpu.make_async_remote_copy(
            src_ref=swap_out.at[way, j],
            dst_ref=swap_in.at[way, j],
            send_sem=swap_send.at[way, j],
            recv_sem=swap_recv.at[way, j],
            device_id=across,
            device_id_type=MESH,
        )

    last = chips - 2
    parts = [own_part(way, chips) for way in range(2)]
    for j in range(pieces):
        for way in range(2):
            reduce_copy(way, last, j, moving.at[way, last, j]).wait_recv()
            swap_out[way, j] = (
                moving[way, last, j].astype(jnp.float32) + parts[way][j * piece : (j + 1) * piece]
            ).astype(jnp.bfloat16)
            swap_copy(way, j).start()

    def gather_copy(way, step, j):
        index = chunk(way, chips + step if way == 1 else step)
        return pltpu.make_async_remote_copy(
            src_ref=hidden.at[index, way, j],
            dst_ref=hidden.at[index, way, j],
            send_sem=gather_send.at[way, step, j],
            recv_sem=gather_recv.at[way, step, j],
            device_id=ways[way],
            device_id_type=MESH,
        )

    for j in range(pieces):
        for way in range(2):
            swap_copy(way, j).wait_recv()
            hidden[place, way, j] = (
                swap_out[way, j].astype(jnp.float32) + swap_in[way, j].astype(jnp.float32)
            ).astype(jnp.bfloat16)
            gather_copy(way, 0, j).start()

    ones = jnp.ones((8, half), jnp.float32)
    squares = []
    for j in range(pieces):
        total = None
        for way in range(2):
            value = hidden[place, way, j].astype(jnp.float32)
            total = value * value if total is None else total + value * value
        squares.append(
            lax.dot_general(
                ones,
                total,
                (((1,), (1,)), ((), ())),
                preferred_element_type=jnp.float32,
                precision=lax.Precision.HIGHEST,
            )
        )
    is_along = lax.broadcasted_iota(jnp.int32, (8, tokens), 0) == 0
    own_stats[...] = jnp.where(is_along, along, 0.5 * jnp.concatenate(squares, axis=1))

    def stats_copy(k):
        return pltpu.make_async_remote_copy(
            src_ref=own_stats,
            dst_ref=far_stats.at[k],
            send_sem=stats_send.at[k],
            recv_sem=stats_recv.at[k],
            device_id=(seq, lax.rem(tensor + k, tensor_count)),
            device_id_type=MESH,
        )

    def reward_copy(k):
        return pltpu.make_async_remote_copy(
            src_ref=own_reward,
            dst_ref=rewards_ref.at[seq],
            send_sem=reward_send.at[k],
            recv_sem=reward_recv.at[k],
            device_id=(lax.rem(seq + k, seq_count), tensor),
            device_id_type=MESH,
        )

    def start_stats(k, _):
        stats_copy(k).start()
        return 0

    lax.fori_loop(1, tensor_count, start_stats, 0)

    def back_part(index, way):
        return lax.dot_general(
            hidden[index, way].reshape(tokens, half),
            weight_ref[rows(index, way), :],
            (((1,), (0,)), ((), ())),
            preferred_element_type=jnp.float32,
        )

    back_ref[...] = back_part(place, 0) + back_part(place, 1)

    def gather_step(step, _):
        for j in range(pieces):
            for way in range(2):
                gather_copy(way, step, j).wait_recv()
                gather_copy(way, step + 1, j).start()
        back_ref[...] += back_part(chunk(0, step + 1), 0) + back_part(chunk(1, step + 1), 1)
        return 0

    lax.fori_loop(0, 2, gather_step, 0)

    def add_stats(k, total):
        stats_copy(k).wait_recv()
        return total + far_stats[k]

    stats = lax.fori_loop(1, tensor_count, add_stats, own_stats[...])
    stats_ref[...] = stats
    scale = jnp.sqrt(stats[1:2] / model_width + norm_eps)
    own_reward[...] = jnp.broadcast_to(stats[0:1] / scale, own_reward.shape)
    rewards_ref[seq] = own_reward[...]

    def start_reward(k, _):
        reward_copy(k).start()
        return 0

    lax.fori_loop(1, seq_count, start_reward, 0)
    lax.fori_loop(2, chips - 2, gather_step, 0)
    for j in range(pieces):
        for way in range(2):
            gather_copy(way, last, j).wait_recv()
    back_ref[...] += back_part(chunk(0, chips - 1), 0) + back_part(chunk(1, chips - 1), 1)

    def end_reward(k, _):
        reward_copy(k).wait()
        return 0

    lax.fori_loop(1, seq_count, end_reward, 0)

    def end_stats(k, _):
        stats_copy(k).wait_send()
        return 0

    lax.fori_loop(1, tensor_count, end_stats, 0)

    def end_ring(step, _):
        for j in range(pieces):
            for way in range(2):
                reduce_copy(way, step, j, first.at[way, j]).wait_send()
                gather_copy(way, step, j).wait_send()
        return 0

    lax.fori_loop(0, chips - 1, end_ring, 0)
    for j in range(pieces):
        for way in range(2):
            swap_copy(way, j).wait_send()


def exchange(mixed, weight, reward_channels):
    tokens, channels = mixed.shape
    model_width = weight.shape[0]
    chips = lax.axis_size("tensor") // 2
    seq_count, tensor_count = lax.axis_size("seq"), lax.axis_size("tensor")
    half = model_width // (2 * chips)
    pieces = 2
    piece = tokens // pieces
    vmem = pl.BlockSpec(memory_space=pltpu.VMEM)
    steps = chips - 1
    return pl.pallas_call(
        exchange_kernel,
        out_shape=(
            jax.ShapeDtypeStruct((tokens, channels), jnp.float32),
            jax.ShapeDtypeStruct((8, tokens), jnp.float32),
            jax.ShapeDtypeStruct((seq_count, 8, tokens), jnp.float32),
        ),
        in_specs=[vmem] * 3,
        out_specs=(vmem,) * 3,
        scratch_shapes=[
            pltpu.VMEM((2, pieces, piece, half), jnp.bfloat16),
            pltpu.VMEM((2, steps, pieces, piece, half), jnp.bfloat16),
            pltpu.VMEM((2, pieces, piece, half), jnp.bfloat16),
            pltpu.VMEM((2, pieces, piece, half), jnp.bfloat16),
            pltpu.VMEM((chips, 2, pieces, piece, half), jnp.bfloat16),
            pltpu.VMEM((8, tokens), jnp.float32),
            pltpu.VMEM((tensor_count, 8, tokens), jnp.float32),
            pltpu.VMEM((8, tokens), jnp.float32),
            pltpu.SemaphoreType.DMA((2, steps, pieces)),
            pltpu.SemaphoreType.DMA((2, steps, pieces)),
            pltpu.SemaphoreType.DMA((2, pieces)),
            pltpu.SemaphoreType.DMA((2, pieces)),
            pltpu.SemaphoreType.DMA((2, steps, pieces)),
            pltpu.SemaphoreType.DMA((2, steps, pieces)),
            pltpu.SemaphoreType.DMA((tensor_count,)),
            pltpu.SemaphoreType.DMA((tensor_count,)),
            pltpu.SemaphoreType.DMA((seq_count,)),
            pltpu.SemaphoreType.DMA((seq_count,)),
        ],
        compiler_params=pltpu.CompilerParams(
            collective_id=0, has_side_effects=True, vmem_limit_bytes=40 << 20
        ),
        name="exchange",
    )(mixed, weight, reward_channels)


def on_device(
    ssd_input,
    gate_input,
    state_maps,
    step_raw,
    step_bias,
    decay_rate,
    skip_gain,
    norm_gain,
    out_weight,
    reward_head,
    traj_lengths,
    step_pairs,
):
    row_count = ssd_input.shape[0]
    head_count = step_raw.shape[1]
    head_width = ssd_input.shape[1] // head_count
    group_count = state_maps.shape[2] // STATE
    model_width = out_weight.shape[0]
    offset = lax.axis_index("seq") * row_count
    positions = offset + jnp.arange(row_count, dtype=jnp.int32)
    openings = jnp.cumsum(traj_lengths) - traj_lengths
    starts = jnp.any(positions[:, None] == openings[None, :], axis=1).astype(jnp.float32)
    x_heads = ssd_input.astype(jnp.float32).reshape(row_count, head_count, head_width)
    z_heads = gate_input.astype(jnp.float32).reshape(row_count, head_count, head_width)
    b_rows = state_maps[:, 0].astype(jnp.float32).reshape(row_count, group_count, STATE)
    c_rows = state_maps[:, 1].astype(jnp.float32).reshape(row_count, group_count, STATE)

    def state_part(a_in, b_in, c_in):
        return local_state(a_in, b_in, c_in, step_bias, decay_rate, starts)

    (state_local, through), pull_state = jax.vjp(state_part, x_heads, b_rows, step_raw)
    reach = -(-(longest - 1) // row_count)
    state_in = neighbours(through, state_local, "seq", 1, reach)

    def out_part(a_in, b_in, c_in, d_in, e_in, f_in):
        return local_out(
            a_in, b_in, c_in, d_in, e_in, f_in, step_bias, decay_rate, skip_gain, norm_gain, starts
        )

    normed, pull_out = jax.vjp(out_part, x_heads, z_heads, b_rows, c_rows, step_raw, state_in)
    mixed = normed.astype(jnp.bfloat16)
    reward_channels = jnp.sum(out_weight.astype(jnp.float32) * reward_head[:, None], axis=0)
    hidden_back, stats, rewards_far = exchange(mixed, out_weight, reward_channels[None, :])
    own_along, own_squares = stats[0], stats[1]
    own_scale = jnp.sqrt(own_squares / model_width + norm_eps)
    own_rewards = own_along / own_scale
    rewards_all = rewards_far[:, 0].reshape(-1)
    pair_rows = step_pairs.reshape(-1, 2)
    mates = pair_rows[:, ::-1].reshape(1, -1)
    signs = jnp.where(jnp.arange(step_pairs.shape[0]) % 2 == 0, -1.0, 1.0)[None, :]
    hit = positions[:, None] == step_pairs[None, :]
    mate = jnp.sum(jnp.where(hit, mates, 0), axis=1)
    sign = jnp.sum(jnp.where(hit, signs, 0.0), axis=1)
    all_tokens = jnp.arange(step_pairs.shape[0], dtype=jnp.int32)
    mate_reward = jnp.sum(
        jnp.where(mate[:, None] == all_tokens[None, :], rewards_all[None, :], 0.0), axis=1
    )
    own_grad = sign * loss_scale * jax.nn.sigmoid(sign * (own_rewards - mate_reward))
    d_mixed = (own_grad / own_scale)[:, None] * (
        reward_channels[None, :]
        - (own_along / (model_width * own_scale * own_scale))[:, None] * hidden_back
    )
    out_grads = pull_out(d_mixed)
    grad_in = out_grads[5]
    grad_end = neighbours(through, grad_in, "seq", -1, reach)
    state_grads = pull_state((grad_end, jnp.sum(grad_end * state_in, axis=(1, 2))))
    grad_input = (
        (out_grads[0] + state_grads[0])
        .reshape(row_count, head_count * head_width)
        .astype(jnp.bfloat16)
    )
    grad_gate = out_grads[1].reshape(row_count, head_count * head_width).astype(jnp.bfloat16)
    grad_b = (out_grads[2] + state_grads[1]).reshape(row_count, group_count * STATE)
    grad_c = out_grads[3].reshape(row_count, group_count * STATE)
    grad_maps = jnp.stack([grad_b, grad_c], axis=1).astype(jnp.bfloat16)
    grad_step = out_grads[4] + state_grads[2]
    return (own_rewards, grad_input, grad_gate, grad_maps, grad_step)


def solution(mesh):
    return jax.shard_map(
        on_device,
        mesh=mesh,
        in_specs=(
            P("seq", "tensor"),
            P("seq", "tensor"),
            P("seq", None, "tensor"),
            P("seq", "tensor"),
            P("tensor"),
            P("tensor"),
            P("tensor"),
            P("tensor"),
            P(None, "tensor"),
            P(),
            P(),
            P(),
        ),
        out_specs=(
            P("seq"),
            P("seq", "tensor"),
            P("seq", "tensor"),
            P("seq", None, "tensor"),
            P("seq", "tensor"),
        ),
        check_vma=False,
    )
```

```python
import jax
import jax.numpy as jnp
from jax import lax
from jax.experimental import pallas as pl
from jax.experimental.pallas import tpu as pltpu
from jax.sharding import PartitionSpec as P

STATE = 128
BLOCK = 128

norm_eps = 1e-05
loss_scale = 64.0
longest = 1152
MESH = pl.DeviceIdType.MESH
HIGH = lax.Precision.HIGHEST
NT = ((1,), (1,))
NN = ((1,), (0,))
TN = ((0,), (0,))


def dot(left, right, dims, precision=None):
    return lax.dot_general(
        left, right, (dims, ((), ())), preferred_element_type=jnp.float32, precision=precision
    )


def iota(shape, axis):
    return lax.broadcasted_iota(jnp.int32, shape, axis)


def layer_kernel(
    x_ref,
    z_ref,
    b_ref,
    c_ref,
    raw_ref,
    bias_ref,
    rate_ref,
    wide_ref,
    weight_ref,
    head_ref,
    length_row_ref,
    length_col_ref,
    pairs_ref,
    reward_out,
    dx_ref,
    dz_ref,
    db_ref,
    dc_ref,
    dstep_ref,
    weight,
    columns,
    decays,
    scores,
    y_all,
    carried_all,
    state_in,
    mixed,
    weighted_x,
    mate_all,
    sign_all,
    state_out,
    state_far,
    grad_out,
    grad_far,
    dy_all,
    faded_dy,
    dx_all,
    db_all,
    sums,
    column_sums,
    back,
    rewards,
    first,
    moving,
    swap_out,
    swap_in,
    hidden,
    own_stats,
    far_stats,
    own_reward,
    weight_sem,
    state_send,
    state_recv,
    grad_send,
    grad_recv,
    reduce_send,
    reduce_recv,
    swap_send,
    swap_recv,
    gather_send,
    gather_recv,
    stats_send,
    stats_recv,
    reward_send,
    reward_recv,
):
    seq, tensor = lax.axis_index("seq"), lax.axis_index("tensor")
    seq_count, tensor_count = lax.axis_size("seq"), lax.axis_size("tensor")
    chips = tensor_count // 2
    place, side = lax.rem(tensor, chips), tensor // chips
    base = side * chips
    up = (seq, base + lax.rem(place + 1, chips))
    down = (seq, base + lax.rem(place + chips - 1, chips))
    across = (seq, (1 - side) * chips + place)
    ways = (up, down)
    tokens, channels = x_ref.shape
    model_width = weight.shape[0]
    half = hidden.shape[-1]
    pieces = hidden.shape[2]
    piece = tokens // pieces
    width = channels // (raw_ref.shape[0] // 2)
    heads = channels // width
    blocks = tokens // BLOCK
    reach = state_far.shape[0]
    pair_tiles = pairs_ref.shape[1] // BLOCK

    weight_copy = pltpu.make_async_copy(weight_ref, weight, weight_sem)
    weight_copy.start()
    barrier = pltpu.get_barrier_semaphore()

    def greet_tensor(k, _):
        other = lax.rem(tensor + k, tensor_count)
        pl.semaphore_signal(barrier, inc=1, device_id=(seq, other), device_id_type=MESH)
        return 0

    def greet_seq(k, _):
        other = lax.rem(seq + k, seq_count)
        pl.semaphore_signal(barrier, inc=1, device_id=(other, tensor), device_id_type=MESH)
        return 0

    lax.fori_loop(1, tensor_count, greet_tensor, 0)
    lax.fori_loop(1, seq_count, greet_seq, 0)

    def span(tb):
        return slice(tb * BLOCK, (tb + 1) * BLOCK)

    def lanes(h):
        return slice(h * width, (h + 1) * width)

    pre = raw_ref[...] + bias_ref[...]
    step = jnp.maximum(pre, 0.0) + jnp.log1p(jnp.exp(-jnp.abs(pre)))
    exponent = -step * rate_ref[...]
    square = (tokens, tokens)
    upto = (iota(square, 0) <= iota(square, 1)).astype(jnp.float32)
    cumulative = dot(exponent, upto, NN, HIGH)
    count = length_row_ref.shape[1]
    openings = jnp.sum(
        jnp.where(
            iota((count, count), 1) < iota((count, count), 0),
            length_row_ref[...].astype(jnp.float32),
            0.0,
        ),
        axis=1,
        keepdims=True,
    )
    position = (iota((count, tokens), 1) + seq * tokens).astype(jnp.float32)
    block_start = (iota((count, tokens), 0) * 0 + seq * tokens).astype(jnp.float32)
    segment = jnp.sum(
        jnp.where((openings <= position) & (openings >= block_start), 1.0, 0.0),
        axis=0,
        keepdims=True,
    )
    last_segment = segment[:, tokens - 1 :]
    last_cumulative = cumulative[:, tokens - 1 :]
    end_weight = jnp.where(
        jnp.broadcast_to(segment == last_segment, step.shape),
        jnp.exp(last_cumulative - cumulative),
        0.0,
    )
    end_weight = end_weight * step
    first_weight = jnp.where(
        jnp.broadcast_to(segment == 0.0, step.shape), jnp.exp(cumulative), 0.0
    )
    through = jnp.where(last_segment == 0.0, jnp.exp(last_cumulative), 0.0)
    segment_rows = jnp.broadcast_to(segment, step.shape)
    columns[...] = jnp.concatenate(
        [
            end_weight,
            first_weight,
            cumulative,
            segment_rows,
            jnp.zeros((BLOCK - 32, tokens), jnp.float32),
        ],
        axis=0,
    ).T

    def column(kind, h, tb):
        return columns[span(tb), kind * 8 + h : kind * 8 + h + 1]

    def expanded(kind, tb):
        return jnp.concatenate(
            [jnp.broadcast_to(column(kind, h, tb), (BLOCK, width)) for h in range(heads)], axis=1
        )

    through_wide = jnp.concatenate(
        [jnp.broadcast_to(through[h : h + 1], (1, width)) for h in range(heads)], axis=1
    )
    through_high = through_wide.astype(jnp.bfloat16).astype(jnp.float32)
    tail_shape = (16, channels)
    through_rows = jnp.where(
        iota(tail_shape, 0) == 0,
        through_high,
        jnp.where(iota(tail_shape, 0) == 1, through_wide - through_high, 0.0),
    ).astype(jnp.bfloat16)

    def far_copy(source, target, send, recv, distance, direction):
        return pltpu.make_async_remote_copy(
            src_ref=source,
            dst_ref=target.at[distance - 1],
            send_sem=send.at[distance - 1],
            recv_sem=recv.at[distance - 1],
            device_id=(lax.rem(seq + seq_count + direction * distance, seq_count), tensor),
            device_id_type=MESH,
        )

    def state_copy(distance):
        return far_copy(state_out, state_far, state_send, state_recv, distance, 1)

    def grad_copy(distance):
        return far_copy(grad_out, grad_far, grad_send, grad_recv, distance, -1)

    def gathered(far):
        total, carry = None, None
        for k in range(reach):
            value = far[k, 0:STATE].astype(jnp.float32)
            passed = far[k, STATE : STATE + 1].astype(jnp.float32) + far[
                k, STATE + 1 : STATE + 2
            ].astype(jnp.float32)
            if total is None:
                total, carry = value, passed
            else:
                total = total + carry * value
                carry = carry * passed
        return total

    for tb in range(blocks):
        weighted_x[span(tb)] = (
            x_ref[span(tb)].astype(jnp.float32) * expanded(0, tb)
        ).astype(jnp.bfloat16)
    state_out[0:STATE] = dot(b_ref[...], weighted_x[...], TN).astype(jnp.bfloat16)
    state_out[STATE:] = through_rows
    pl.semaphore_wait(barrier, tensor_count + seq_count - 2)
    for distance in range(1, reach + 1):
        state_copy(distance).start()

    for tb in range(blocks):
        reached = (tb + 1) * BLOCK
        score = dot(c_ref[span(tb)], b_ref[0:reached], NT)
        scores[span(tb), 0:reached] = score
        shape = (BLOCK, reached)
        allowed = (column(3, 0, tb) == segment[:, 0:reached]) & (
            iota(shape, 1) <= iota(shape, 0) + tb * BLOCK
        )
        for h in range(heads):
            spread = column(2, h, tb) - cumulative[h : h + 1, 0:reached]
            decay = jnp.exp(jnp.where(allowed, spread, -1e30)) * step[h : h + 1, 0:reached]
            decays[h, span(tb), 0:reached] = decay
            y_all[span(tb), lanes(h)] = dot(
                (decay * score).astype(jnp.bfloat16), x_ref[0:reached, lanes(h)], NN
            )

    reward_row = head_ref[...]
    high = reward_row.astype(jnp.bfloat16).astype(jnp.float32)
    rest = reward_row - high
    middle = rest.astype(jnp.bfloat16).astype(jnp.float32)
    term = iota((8, model_width), 0)
    terms = jnp.where(
        term == 0,
        high,
        jnp.where(term == 1, middle, jnp.where(term == 2, rest - middle, 0.0)),
    ).astype(jnp.bfloat16)
    weight_copy.wait()
    reward_channels = jnp.sum(dot(terms, weight[...], NN), axis=0, keepdims=True)

    tile = (BLOCK, BLOCK)
    unroll = 4
    for tb in range(blocks):
        token = iota(tile, 0) + (seq * tokens + tb * BLOCK)

        def find(i, total):
            for k in range(unroll):
                start = pl.multiple_of((i * unroll + k) * BLOCK, BLOCK)
                row = pairs_ref[0:1, pl.ds(start, BLOCK)]
                order = (iota(tile, 1) + start).astype(jnp.float32)
                total = total + jnp.where(row == token, order, 0.0)
            return total

        zero = jnp.zeros(tile, jnp.float32)
        order = jnp.sum(
            lax.fori_loop(0, pair_tiles // unroll, find, zero), axis=1, keepdims=True
        )
        odd = order - 2.0 * jnp.floor(order * 0.5)
        other = jnp.broadcast_to(order + 1.0 - 2.0 * odd, tile)

        def fetch(i, total):
            for k in range(unroll):
                start = pl.multiple_of((i * unroll + k) * BLOCK, BLOCK)
                row = pairs_ref[0:1, pl.ds(start, BLOCK)].astype(jnp.float32)
                order = (iota(tile, 1) + start).astype(jnp.float32)
                total = total + jnp.where(other == order, row, 0.0)
            return total

        mate = jnp.sum(
            lax.fori_loop(0, pair_tiles // unroll, fetch, zero), axis=1, keepdims=True
        )
        mate_all[span(tb)] = jnp.broadcast_to(mate, tile)
        sign_all[span(tb)] = jnp.broadcast_to(2.0 * odd - 1.0, tile)

    for distance in range(1, reach + 1):
        state_copy(distance).wait_recv()
    state_in[...] = gathered(state_far)
    incoming = state_in[...].astype(jnp.bfloat16)
    gain, skip = wide_ref[0:1], wide_ref[1:2]

    def gating(tb):
        y = y_all[span(tb)]
        z = z_ref[span(tb)].astype(jnp.float32)
        sig = 1.0 / (1.0 + jnp.exp(-z))
        silu = z * sig
        gated = y * silu
        mean_square = jnp.sum(gated * gated, axis=1, keepdims=True) / channels
        return y, z, sig, silu, gated, lax.rsqrt(mean_square + norm_eps)

    for tb in range(blocks):
        carried = expanded(1, tb) * dot(c_ref[span(tb)], incoming, NN)
        carried_all[span(tb)] = carried
        y_all[span(tb)] = (
            y_all[span(tb)] + carried + skip * x_ref[span(tb)].astype(jnp.float32)
        )
        _, _, _, _, gated, inverse = gating(tb)
        mixed[span(tb)] = (gated * inverse * gain).astype(jnp.bfloat16)

    def chunk(way, distance):
        move = distance if way == 1 else chips - distance
        return lax.rem(place + move, chips)

    def rows(index, way):
        return pl.ds(pl.multiple_of((index * 2 + way) * half, half), half)

    def own_part(way, distance):
        return lax.dot_general(
            mixed[...],
            weight[rows(chunk(way, distance), way), :],
            (((1,), (1,)), ((), ())),
            preferred_element_type=jnp.float32,
        )

    def reduce_copy(way, step, j, source):
        return pltpu.make_async_remote_copy(
            src_ref=source,
            dst_ref=moving.at[way, step, j],
            send_sem=reduce_send.at[way, step, j],
            recv_sem=reduce_recv.at[way, step, j],
            device_id=ways[way],
            device_id_type=MESH,
        )

    def reduce_source(way, step, j):
        return first.at[way, j] if step is None else moving.at[way, step, j]

    for way in range(2):
        part = own_part(way, 1)
        for j in range(pieces):
            first[way, j] = part[j * piece : (j + 1) * piece].astype(jnp.bfloat16)
    for j in range(pieces):
        for way in range(2):
            reduce_copy(way, 0, j, first.at[way, j]).start()

    along = lax.dot_general(
        jnp.broadcast_to(reward_channels, (8, channels)),
        mixed[...].astype(jnp.float32),
        (((1,), (1,)), ((), ())),
        preferred_element_type=jnp.float32,
        precision=lax.Precision.HIGHEST,
    )

    def reduce_step(step, _):
        parts = [own_part(way, step + 2) for way in range(2)]
        for j in range(pieces):
            for way in range(2):
                reduce_copy(way, step, j, moving.at[way, step, j]).wait_recv()
                moving[way, step, j] = (
                    moving[way, step, j].astype(jnp.float32)
                    + parts[way][j * piece : (j + 1) * piece]
                ).astype(jnp.bfloat16)
                reduce_copy(way, step + 1, j, moving.at[way, step, j]).start()
        return 0

    lax.fori_loop(0, chips - 2, reduce_step, 0)

    def swap_copy(way, j):
        return pltpu.make_async_remote_copy(
            src_ref=swap_out.at[way, j],
            dst_ref=swap_in.at[way, j],
            send_sem=swap_send.at[way, j],
            recv_sem=swap_recv.at[way, j],
            device_id=across,
            device_id_type=MESH,
        )

    last = chips - 2
    parts = [own_part(way, chips) for way in range(2)]
    for j in range(pieces):
        for way in range(2):
            reduce_copy(way, last, j, moving.at[way, last, j]).wait_recv()
            swap_out[way, j] = (
                moving[way, last, j].astype(jnp.float32) + parts[way][j * piece : (j + 1) * piece]
            ).astype(jnp.bfloat16)
            swap_copy(way, j).start()

    def gather_copy(way, step, j):
        index = chunk(way, chips + step if way == 1 else step)
        return pltpu.make_async_remote_copy(
            src_ref=hidden.at[index, way, j],
            dst_ref=hidden.at[index, way, j],
            send_sem=gather_send.at[way, step, j],
            recv_sem=gather_recv.at[way, step, j],
            device_id=ways[way],
            device_id_type=MESH,
        )

    for j in range(pieces):
        for way in range(2):
            swap_copy(way, j).wait_recv()
            hidden[place, way, j] = (
                swap_out[way, j].astype(jnp.float32) + swap_in[way, j].astype(jnp.float32)
            ).astype(jnp.bfloat16)
            gather_copy(way, 0, j).start()

    ones = jnp.ones((8, half), jnp.float32)
    squares = []
    for j in range(pieces):
        total = None
        for way in range(2):
            value = hidden[place, way, j].astype(jnp.float32)
            total = value * value if total is None else total + value * value
        squares.append(
            lax.dot_general(
                ones,
                total,
                (((1,), (1,)), ((), ())),
                preferred_element_type=jnp.float32,
                precision=lax.Precision.HIGHEST,
            )
        )
    is_along = lax.broadcasted_iota(jnp.int32, (8, tokens), 0) == 0
    own_stats[...] = jnp.where(is_along, along, 0.5 * jnp.concatenate(squares, axis=1))

    def stats_copy(k):
        return pltpu.make_async_remote_copy(
            src_ref=own_stats,
            dst_ref=far_stats.at[k],
            send_sem=stats_send.at[k],
            recv_sem=stats_recv.at[k],
            device_id=(seq, lax.rem(tensor + k, tensor_count)),
            device_id_type=MESH,
        )

    def reward_copy(k):
        return pltpu.make_async_remote_copy(
            src_ref=own_reward,
            dst_ref=rewards.at[seq],
            send_sem=reward_send.at[k],
            recv_sem=reward_recv.at[k],
            device_id=(lax.rem(seq + k, seq_count), tensor),
            device_id_type=MESH,
        )

    def start_stats(k, _):
        stats_copy(k).start()
        return 0

    lax.fori_loop(1, tensor_count, start_stats, 0)

    def back_part(index, way):
        return lax.dot_general(
            hidden[index, way].reshape(tokens, half),
            weight[rows(index, way), :],
            (((1,), (0,)), ((), ())),
            preferred_element_type=jnp.float32,
        )

    back[...] = back_part(place, 0) + back_part(place, 1)

    def gather_step(step, _):
        for j in range(pieces):
            for way in range(2):
                gather_copy(way, step, j).wait_recv()
                gather_copy(way, step + 1, j).start()
        back[...] += back_part(chunk(0, step + 1), 0) + back_part(chunk(1, step + 1), 1)
        return 0

    lax.fori_loop(0, 2, gather_step, 0)

    def add_stats(k, total):
        stats_copy(k).wait_recv()
        return total + far_stats[k]

    stats = lax.fori_loop(1, tensor_count, add_stats, own_stats[...])
    scale = jnp.sqrt(stats[1:2] / model_width + norm_eps)
    own_reward[...] = jnp.broadcast_to(stats[0:1] / scale, own_reward.shape)
    rewards[seq] = own_reward[...]

    def start_reward(k, _):
        reward_copy(k).start()
        return 0

    lax.fori_loop(1, seq_count, start_reward, 0)
    lax.fori_loop(2, chips - 2, gather_step, 0)
    for j in range(pieces):
        for way in range(2):
            gather_copy(way, last, j).wait_recv()
    back[...] += back_part(chunk(0, chips - 1), 0) + back_part(chunk(1, chips - 1), 1)

    def end_reward(k, _):
        reward_copy(k).wait()
        return 0

    lax.fori_loop(1, seq_count, end_reward, 0)

    def end_stats(k, _):
        stats_copy(k).wait_send()
        return 0

    lax.fori_loop(1, tensor_count, end_stats, 0)

    def end_ring(step, _):
        for j in range(pieces):
            for way in range(2):
                reduce_copy(way, step, j, first.at[way, j]).wait_send()
                gather_copy(way, step, j).wait_send()
        return 0

    lax.fori_loop(0, chips - 1, end_ring, 0)
    for j in range(pieces):
        for way in range(2):
            swap_copy(way, j).wait_send()

    reward_out[...] = own_reward[...]

    facts = jnp.concatenate(
        [stats, jnp.broadcast_to(scale, stats.shape), own_reward[...]]
        + [jnp.zeros((BLOCK - 24, tokens), jnp.float32)],
        axis=0,
    ).T
    lane = iota(tile, 1)
    for tb in range(blocks):
        mate = mate_all[span(tb)].astype(jnp.int32)
        sign = sign_all[span(tb), 0:1]

        def look(i, total):
            for k in range(blocks):
                row = rewards[i, 0:1, k * BLOCK : (k + 1) * BLOCK]
                total = total + jnp.where(mate == lane + (i * tokens + k * BLOCK), row, 0.0)
            return total

        mate_reward = jnp.sum(
            lax.fori_loop(0, seq_count, look, jnp.zeros(tile, jnp.float32)), axis=1, keepdims=True
        )
        own_along = facts[span(tb), 0:1]
        own_scale = facts[span(tb), 8:9]
        push = sign * (facts[span(tb), 16:17] - mate_reward)
        pair_grad = sign * (loss_scale / (1.0 + jnp.exp(-push)))
        y, z, sig, silu, gated, inverse = gating(tb)
        d_gained = gain * (
            (pair_grad / own_scale)
            * (reward_channels - (own_along / (model_width * own_scale * own_scale)) * back[span(tb)])
        )
        shared = jnp.sum(gated * d_gained, axis=1, keepdims=True) / channels
        d_gated = inverse * d_gained - gated * (inverse * inverse * inverse * shared)
        dz_ref[span(tb)] = (d_gated * y * (sig * (1.0 + z * (1.0 - sig)))).astype(jnp.bfloat16)
        dy = d_gated * silu
        dy_all[span(tb)] = dy.astype(jnp.bfloat16)
        faded_dy[span(tb)] = (dy * expanded(1, tb)).astype(jnp.bfloat16)
        dx_all[span(tb)] = skip * dy
        product = dy * carried_all[span(tb)]
        total = jnp.zeros(tile, jnp.float32)
        for h in range(heads):
            total = total + jnp.where(
                lane == h, jnp.sum(product[:, lanes(h)], axis=1, keepdims=True), 0.0
            )
        sums[span(tb)] = total
    grad_out[0:STATE] = dot(c_ref[...], faded_dy[...], TN).astype(jnp.bfloat16)
    grad_out[STATE:] = through_rows
    for distance in range(1, reach + 1):
        grad_copy(distance).start()

    column_sums[...] = jnp.zeros_like(column_sums)
    db_all[...] = jnp.zeros_like(db_all)
    for tb in range(blocks):
        reached = (tb + 1) * BLOCK
        score = scores[span(tb), 0:reached]
        d_score = None
        row_sums = sums[span(tb)]
        for h in range(heads):
            dy = dy_all[span(tb), lanes(h)]
            decay = decays[h, span(tb), 0:reached]
            d_decayed = decay * dot(dy, x_ref[0:reached, lanes(h)], NT)
            d_score = d_decayed if d_score is None else d_score + d_decayed
            weighed = d_decayed * score
            row_sums = row_sums + jnp.where(
                lane == h, jnp.sum(weighed, axis=1, keepdims=True), 0.0
            )
            column_sums[h : h + 1, 0:reached] += jnp.sum(weighed, axis=0, keepdims=True)
            dx_all[0:reached, lanes(h)] += dot((decay * score).astype(jnp.bfloat16), dy, TN)
        sums[span(tb)] = row_sums
        d_score = d_score.astype(jnp.bfloat16)
        dc_ref[span(tb)] = (
            dot(d_score, b_ref[0:reached], NN) + dot(faded_dy[span(tb)], incoming, NT)
        ).astype(jnp.bfloat16)
        db_all[0:reached] += dot(d_score, c_ref[span(tb)], TN)

    for distance in range(1, reach + 1):
        grad_copy(distance).wait_recv()
    grad_end = gathered(grad_far)
    crossing = jnp.sum(grad_end * state_in[...], axis=0, keepdims=True)
    grad_end = grad_end.astype(jnp.bfloat16)
    for tb in range(blocks):
        d_weighted = expanded(0, tb) * dot(b_ref[span(tb)], grad_end, NN)
        dx_ref[span(tb)] = (dx_all[span(tb)] + d_weighted).astype(jnp.bfloat16)
        db_ref[span(tb)] = (
            db_all[span(tb)] + dot(weighted_x[span(tb)], grad_end, NT)
        ).astype(jnp.bfloat16)
        product = d_weighted * x_ref[span(tb)].astype(jnp.float32)
        total = sums[span(tb)]
        for h in range(heads):
            total = total + jnp.where(
                lane == h + 8, jnp.sum(product[:, lanes(h)], axis=1, keepdims=True), 0.0
            )
        sums[span(tb)] = total
    turned = sums[...].T
    weight_sums = turned[8:16]
    reach_end = jnp.zeros((8, 1), jnp.float32)
    for h in range(heads):
        reach_end = reach_end + jnp.where(
            iota((8, 1), 0) == h, jnp.sum(crossing[:, lanes(h)], axis=1, keepdims=True), 0.0
        )
    d_last = jnp.sum(weight_sums, axis=1, keepdims=True) + through * reach_end
    d_cumulative = turned[0:8] - column_sums[...] - weight_sums
    d_cumulative = d_cumulative + jnp.where(iota(step.shape, 1) == tokens - 1, d_last, 0.0)
    onward = (iota(square, 0) >= iota(square, 1)).astype(jnp.float32)
    d_exponent = dot(d_cumulative, onward, NN, HIGH)
    d_step = (column_sums[...] + weight_sums) / step - rate_ref[...] * d_exponent
    dstep_ref[...] = d_step / (1.0 + jnp.exp(-pre))

    for distance in range(1, reach + 1):
        state_copy(distance).wait_send()
        grad_copy(distance).wait_send()


def on_device(
    ssd_input,
    gate_input,
    state_maps,
    step_raw,
    step_bias,
    decay_rate,
    skip_gain,
    norm_gain,
    out_weight,
    reward_head,
    traj_lengths,
    step_pairs,
):
    tokens, channels = ssd_input.shape
    heads = step_raw.shape[1]
    model_width = out_weight.shape[0]
    seq_count, tensor_count = lax.axis_size("seq"), lax.axis_size("tensor")
    chips = tensor_count // 2
    half = model_width // (2 * chips)
    pieces = 2
    piece = tokens // pieces
    steps = chips - 1
    reach = -(-(longest - 1) // tokens)
    bf16, f32 = jnp.bfloat16, jnp.float32

    def twice(value):
        return jnp.concatenate([value, value], axis=0)

    wide = jnp.concatenate(
        [norm_gain[None, :], jnp.repeat(skip_gain, channels // heads)[None, :]]
        + [jnp.zeros((6, channels), f32)],
        axis=0,
    )
    operands = (
        ssd_input,
        gate_input,
        state_maps[:, 0],
        state_maps[:, 1],
        twice(step_raw.T),
        twice(step_bias)[:, None],
        twice(decay_rate)[:, None],
        wide,
        out_weight,
        reward_head[None, :],
        traj_lengths[None, :],
        traj_lengths[:, None],
        step_pairs[None, :],
    )
    vmem = pl.BlockSpec(memory_space=pltpu.VMEM)
    in_specs = [vmem] * len(operands)
    in_specs[8] = pl.BlockSpec(memory_space=pl.ANY)
    rewards, dx, dz, db, dc, dstep = pl.pallas_call(
        layer_kernel,
        out_shape=(
            jax.ShapeDtypeStruct((8, tokens), f32),
            jax.ShapeDtypeStruct((tokens, channels), bf16),
            jax.ShapeDtypeStruct((tokens, channels), bf16),
            jax.ShapeDtypeStruct((tokens, STATE), bf16),
            jax.ShapeDtypeStruct((tokens, STATE), bf16),
            jax.ShapeDtypeStruct((8, tokens), f32),
        ),
        in_specs=in_specs,
        out_specs=(vmem,) * 6,
        scratch_shapes=[
            pltpu.VMEM((model_width, channels), bf16),
            pltpu.VMEM((tokens, BLOCK), f32),
            pltpu.VMEM((heads, tokens, tokens), f32),
            pltpu.VMEM((tokens, tokens), f32),
            pltpu.VMEM((tokens, channels), f32),
            pltpu.VMEM((tokens, channels), f32),
            pltpu.VMEM((STATE, channels), f32),
            pltpu.VMEM((tokens, channels), bf16),
            pltpu.VMEM((tokens, channels), bf16),
            pltpu.VMEM((tokens, BLOCK), f32),
            pltpu.VMEM((tokens, BLOCK), f32),
            pltpu.VMEM((STATE + 16, channels), bf16),
            pltpu.VMEM((reach, STATE + 16, channels), bf16),
            pltpu.VMEM((STATE + 16, channels), bf16),
            pltpu.VMEM((reach, STATE + 16, channels), bf16),
            pltpu.VMEM((tokens, channels), bf16),
            pltpu.VMEM((tokens, channels), bf16),
            pltpu.VMEM((tokens, channels), f32),
            pltpu.VMEM((tokens, STATE), f32),
            pltpu.VMEM((tokens, BLOCK), f32),
            pltpu.VMEM((8, tokens), f32),
            pltpu.VMEM((tokens, channels), f32),
            pltpu.VMEM((seq_count, 8, tokens), f32),
            pltpu.VMEM((2, pieces, piece, half), bf16),
            pltpu.VMEM((2, steps, pieces, piece, half), bf16),
            pltpu.VMEM((2, pieces, piece, half), bf16),
            pltpu.VMEM((2, pieces, piece, half), bf16),
            pltpu.VMEM((chips, 2, pieces, piece, half), bf16),
            pltpu.VMEM((8, tokens), f32),
            pltpu.VMEM((tensor_count, 8, tokens), f32),
            pltpu.VMEM((8, tokens), f32),
            pltpu.SemaphoreType.DMA,
            pltpu.SemaphoreType.DMA((reach,)),
            pltpu.SemaphoreType.DMA((reach,)),
            pltpu.SemaphoreType.DMA((reach,)),
            pltpu.SemaphoreType.DMA((reach,)),
            pltpu.SemaphoreType.DMA((2, steps, pieces)),
            pltpu.SemaphoreType.DMA((2, steps, pieces)),
            pltpu.SemaphoreType.DMA((2, pieces)),
            pltpu.SemaphoreType.DMA((2, pieces)),
            pltpu.SemaphoreType.DMA((2, steps, pieces)),
            pltpu.SemaphoreType.DMA((2, steps, pieces)),
            pltpu.SemaphoreType.DMA((tensor_count,)),
            pltpu.SemaphoreType.DMA((tensor_count,)),
            pltpu.SemaphoreType.DMA((seq_count,)),
            pltpu.SemaphoreType.DMA((seq_count,)),
        ],
        compiler_params=pltpu.CompilerParams(
            collective_id=0, has_side_effects=True, vmem_limit_bytes=48 << 20
        ),
        name="layer",
    )(*operands)
    return (rewards[0], dx, dz, jnp.stack([db, dc], axis=1), dstep[:heads].T)


def solution(mesh):
    return jax.shard_map(
        on_device,
        mesh=mesh,
        in_specs=(
            P("seq", "tensor"),
            P("seq", "tensor"),
            P("seq", None, "tensor"),
            P("seq", "tensor"),
            P("tensor"),
            P("tensor"),
            P("tensor"),
            P("tensor"),
            P(None, "tensor"),
            P(),
            P(),
            P(),
        ),
        out_specs=(
            P("seq"),
            P("seq", "tensor"),
            P("seq", "tensor"),
            P("seq", None, "tensor"),
            P("seq", "tensor"),
        ),
        check_vma=False,
    )
```

```python
import jax
import jax.numpy as jnp
from jax import lax
from jax.experimental import pallas as pl
from jax.experimental.pallas import tpu as pltpu
from jax.sharding import PartitionSpec as P

STATE = 128
BLOCK = 128

norm_eps = 1e-05
loss_scale = 64.0
longest = 1152
MESH = pl.DeviceIdType.MESH
HIGH = lax.Precision.HIGHEST
NT = ((1,), (1,))
NN = ((1,), (0,))
TN = ((0,), (0,))


def dot(left, right, dims, precision=None):
    return lax.dot_general(
        left, right, (dims, ((), ())), preferred_element_type=jnp.float32, precision=precision
    )


def iota(shape, axis):
    return lax.broadcasted_iota(jnp.int32, shape, axis)


def layer_kernel(
    x_hbm,
    z_hbm,
    maps_hbm,
    raw_hbm,
    bias_ref,
    rate_ref,
    skip_ref,
    gain_hbm,
    weight_hbm,
    head_hbm,
    length_hbm,
    pairs_hbm,
    reward_out,
    dx_ref,
    dz_ref,
    dmaps_ref,
    dstep_ref,
    weight,
    x_ref,
    z_ref,
    maps_ref,
    raw_ref,
    gain_ref,
    head_ref,
    length_ref,
    pairs_ref,
    maps_wide,
    b_ref,
    c_ref,
    columns,
    decays,
    scores,
    y_all,
    carried_all,
    state_in,
    mixed,
    weighted_x,
    mate_all,
    sign_all,
    state_out,
    state_far,
    grad_out,
    grad_far,
    dy_all,
    faded_dy,
    dx_all,
    db_all,
    sums,
    column_sums,
    back,
    rewards,
    late_out,
    late_moving,
    swap_out,
    swap_in,
    late_hidden,
    early_out,
    early_moving,
    halve_out,
    halve_in,
    early_hidden,
    own_stats,
    far_stats,
    own_reward,
    load_sems,
    state_send,
    state_recv,
    grad_send,
    grad_recv,
    late_reduce_send,
    late_reduce_recv,
    swap_send,
    swap_recv,
    late_gather_send,
    late_gather_recv,
    early_reduce_send,
    early_reduce_recv,
    early_gather_send,
    early_gather_recv,
    halve_send,
    halve_recv,
    join_send,
    join_recv,
    stats_send,
    stats_recv,
    reward_send,
    reward_recv,
):
    seq, tensor = lax.axis_index("seq"), lax.axis_index("tensor")
    seq_count, tensor_count = lax.axis_size("seq"), lax.axis_size("tensor")
    chips = tensor_count // 2
    place, side = lax.rem(tensor, chips), tensor // chips
    base = side * chips
    up = (seq, base + lax.rem(place + 1, chips))
    down = (seq, base + lax.rem(place + chips - 1, chips))
    across = (seq, (1 - side) * chips + place)
    ways = (up, down)
    tokens, channels = x_ref.shape
    model_width = weight.shape[0]
    late_pieces, piece, late_width = late_hidden.shape[2:]
    early_pieces, _, early_width = early_hidden.shape[3:]
    cut = late_pieces * piece
    width = channels // (raw_ref.shape[0])
    heads = channels // width
    blocks = tokens // BLOCK
    reach = state_far.shape[0]
    pair_tiles = pairs_ref.shape[1] // BLOCK

    loads = [
        pltpu.make_async_copy(source, target, load_sems.at[k])
        for k, (source, target) in enumerate(
            [
                (raw_hbm, raw_ref),
                (length_hbm, length_ref),
                (maps_hbm, maps_ref),
                (x_hbm, x_ref),
                (pairs_hbm, pairs_ref),
                (head_hbm, head_ref),
                (gain_hbm, gain_ref),
                (z_hbm, z_ref),
                (weight_hbm, weight),
            ]
        )
    ]
    for load in loads:
        load.start()
    barrier = pltpu.get_barrier_semaphore()

    def greet_tensor(k, _):
        other = lax.rem(tensor + k, tensor_count)
        pl.semaphore_signal(barrier, inc=1, device_id=(seq, other), device_id_type=MESH)
        return 0

    def greet_seq(k, _):
        other = lax.rem(seq + k, seq_count)
        pl.semaphore_signal(barrier, inc=1, device_id=(other, tensor), device_id_type=MESH)
        return 0

    lax.fori_loop(1, tensor_count, greet_tensor, 0)
    lax.fori_loop(1, seq_count, greet_seq, 0)

    def span(tb):
        return slice(tb * BLOCK, (tb + 1) * BLOCK)

    def lanes(h):
        return slice(h * width, (h + 1) * width)

    def per_head(ref):
        row = lax.rem(iota((8, 1), 0), heads)
        return sum(jnp.where(row == h, ref[h], 0.0) for h in range(heads))

    bias, rate = per_head(bias_ref), per_head(rate_ref)
    for load in loads[:2]:
        load.wait()
    pre = jnp.concatenate([raw_ref[...], raw_ref[...]], axis=0) + bias
    step = jnp.maximum(pre, 0.0) + jnp.log1p(jnp.exp(-jnp.abs(pre)))
    exponent = -step * rate
    square = (tokens, tokens)
    upto = (iota(square, 0) <= iota(square, 1)).astype(jnp.float32)
    cumulative = dot(exponent, upto, NN, HIGH)
    count = length_ref.shape[1]
    openings = jnp.sum(
        jnp.where(
            iota((count, count), 1) < iota((count, count), 0),
            length_ref[...].astype(jnp.float32),
            0.0,
        ),
        axis=1,
        keepdims=True,
    )
    position = (iota((count, tokens), 1) + seq * tokens).astype(jnp.float32)
    block_start = (iota((count, tokens), 0) * 0 + seq * tokens).astype(jnp.float32)
    segment = jnp.sum(
        jnp.where((openings <= position) & (openings >= block_start), 1.0, 0.0),
        axis=0,
        keepdims=True,
    )
    last_segment = segment[:, tokens - 1 :]
    last_cumulative = cumulative[:, tokens - 1 :]
    end_weight = jnp.where(
        jnp.broadcast_to(segment == last_segment, step.shape),
        jnp.exp(last_cumulative - cumulative),
        0.0,
    )
    end_weight = end_weight * step
    first_weight = jnp.where(
        jnp.broadcast_to(segment == 0.0, step.shape), jnp.exp(cumulative), 0.0
    )
    through = jnp.where(last_segment == 0.0, jnp.exp(last_cumulative), 0.0)
    segment_rows = jnp.broadcast_to(segment, step.shape)
    columns[...] = jnp.concatenate(
        [
            end_weight,
            first_weight,
            cumulative,
            segment_rows,
            jnp.zeros((BLOCK - 32, tokens), jnp.float32),
        ],
        axis=0,
    ).T

    def column(kind, h, tb):
        return columns[span(tb), kind * 8 + h : kind * 8 + h + 1]

    def expanded(kind, tb):
        return jnp.concatenate(
            [jnp.broadcast_to(column(kind, h, tb), (BLOCK, width)) for h in range(heads)], axis=1
        )

    through_wide = jnp.concatenate(
        [jnp.broadcast_to(through[h : h + 1], (1, width)) for h in range(heads)], axis=1
    )
    through_high = through_wide.astype(jnp.bfloat16).astype(jnp.float32)
    tail_shape = (16, channels)
    through_rows = jnp.where(
        iota(tail_shape, 0) == 0,
        through_high,
        jnp.where(iota(tail_shape, 0) == 1, through_wide - through_high, 0.0),
    ).astype(jnp.bfloat16)

    def far_copy(source, target, send, recv, distance, direction):
        return pltpu.make_async_remote_copy(
            src_ref=source,
            dst_ref=target.at[distance - 1],
            send_sem=send.at[distance - 1],
            recv_sem=recv.at[distance - 1],
            device_id=(lax.rem(seq + seq_count + direction * distance, seq_count), tensor),
            device_id_type=MESH,
        )

    def state_copy(distance):
        return far_copy(state_out, state_far, state_send, state_recv, distance, 1)

    def grad_copy(distance):
        return far_copy(grad_out, grad_far, grad_send, grad_recv, distance, -1)

    def gathered(far):
        total, carry = None, None
        for k in range(reach):
            value = far[k, 0:STATE].astype(jnp.float32)
            passed = far[k, STATE : STATE + 1].astype(jnp.float32) + far[
                k, STATE + 1 : STATE + 2
            ].astype(jnp.float32)
            if total is None:
                total, carry = value, passed
            else:
                total = total + carry * value
                carry = carry * passed
        return total

    loads[2].wait()
    maps_wide[...] = maps_ref[...].astype(jnp.float32)
    b_ref[...] = maps_wide[pl.ds(0, tokens, stride=2), :].astype(jnp.bfloat16)
    c_ref[...] = maps_wide[pl.ds(1, tokens, stride=2), :].astype(jnp.bfloat16)
    loads[3].wait()
    for tb in range(blocks):
        weighted_x[span(tb)] = (
            x_ref[span(tb)].astype(jnp.float32) * expanded(0, tb)
        ).astype(jnp.bfloat16)
    state_out[0:STATE] = dot(b_ref[...], weighted_x[...], TN).astype(jnp.bfloat16)
    state_out[STATE:] = through_rows
    pl.semaphore_wait(barrier, tensor_count + seq_count - 2)
    for distance in range(1, reach + 1):
        state_copy(distance).start()

    for tb in range(blocks):
        reached = (tb + 1) * BLOCK
        score = dot(c_ref[span(tb)], b_ref[0:reached], NT)
        scores[span(tb), 0:reached] = score
        shape = (BLOCK, reached)
        allowed = (column(3, 0, tb) == segment[:, 0:reached]) & (
            iota(shape, 1) <= iota(shape, 0) + tb * BLOCK
        )
        for h in range(heads):
            spread = column(2, h, tb) - cumulative[h : h + 1, 0:reached]
            decay = jnp.exp(jnp.where(allowed, spread, -1e30)) * step[h : h + 1, 0:reached]
            decays[h, span(tb), 0:reached] = decay
            y_all[span(tb), lanes(h)] = dot(
                (decay * score).astype(jnp.bfloat16), x_ref[0:reached, lanes(h)], NN
            )

    for load in loads[4:8]:
        load.wait()
    reward_row = head_ref[...]
    high = reward_row.astype(jnp.bfloat16).astype(jnp.float32)
    rest = reward_row - high
    middle = rest.astype(jnp.bfloat16).astype(jnp.float32)
    term = iota((8, model_width), 0)
    terms = jnp.where(
        term == 0,
        high,
        jnp.where(term == 1, middle, jnp.where(term == 2, rest - middle, 0.0)),
    ).astype(jnp.bfloat16)
    loads[8].wait()
    reward_channels = jnp.sum(dot(terms, weight[...], NN), axis=0, keepdims=True)

    tile = (BLOCK, BLOCK)
    unroll = 4
    for tb in range(blocks):
        token = iota(tile, 0) + (seq * tokens + tb * BLOCK)

        def find(i, total):
            for k in range(unroll):
                start = pl.multiple_of((i * unroll + k) * BLOCK, BLOCK)
                row = pairs_ref[0:1, pl.ds(start, BLOCK)]
                order = (iota(tile, 1) + start).astype(jnp.float32)
                total = total + jnp.where(row == token, order, 0.0)
            return total

        zero = jnp.zeros(tile, jnp.float32)
        order = jnp.sum(
            lax.fori_loop(0, pair_tiles // unroll, find, zero), axis=1, keepdims=True
        )
        odd = order - 2.0 * jnp.floor(order * 0.5)
        other = jnp.broadcast_to(order + 1.0 - 2.0 * odd, tile)

        def fetch(i, total):
            for k in range(unroll):
                start = pl.multiple_of((i * unroll + k) * BLOCK, BLOCK)
                row = pairs_ref[0:1, pl.ds(start, BLOCK)].astype(jnp.float32)
                order = (iota(tile, 1) + start).astype(jnp.float32)
                total = total + jnp.where(other == order, row, 0.0)
            return total

        mate = jnp.sum(
            lax.fori_loop(0, pair_tiles // unroll, fetch, zero), axis=1, keepdims=True
        )
        mate_all[span(tb)] = jnp.broadcast_to(mate, tile)
        sign_all[span(tb)] = jnp.broadcast_to(2.0 * odd - 1.0, tile)

    for distance in range(1, reach + 1):
        state_copy(distance).wait_recv()
    state_in[...] = gathered(state_far)
    incoming = state_in[...].astype(jnp.bfloat16)
    gain = gain_ref[...]
    skip = jnp.concatenate([jnp.full((1, width), skip_ref[h]) for h in range(heads)], axis=1)

    def gating(tb):
        y = y_all[span(tb)]
        z = z_ref[span(tb)].astype(jnp.float32)
        sig = 1.0 / (1.0 + jnp.exp(-z))
        silu = z * sig
        gated = y * silu
        mean_square = jnp.sum(gated * gated, axis=1, keepdims=True) / channels
        return y, z, sig, silu, gated, lax.rsqrt(mean_square + norm_eps)

    for tb in range(blocks):
        carried = expanded(1, tb) * dot(c_ref[span(tb)], incoming, NN)
        carried_all[span(tb)] = carried
        y_all[span(tb)] = (
            y_all[span(tb)] + carried + skip * x_ref[span(tb)].astype(jnp.float32)
        )
        _, _, _, _, gated, inverse = gating(tb)
        mixed[span(tb)] = (gated * inverse * gain).astype(jnp.bfloat16)

    last = chips - 2

    def chunk(way, distance):
        return lax.rem(place + chips + (distance if way == 0 else -distance), chips)

    def part_half(way, i):
        odd = lax.rem(i, 2)
        return odd if way == 0 else 1 - odd

    def reduce_spot(way, i):
        return chunk(way, chips // 2 - lax.div(i + 1, 2)), part_half(way, i)

    def gather_spot(way, i):
        return chunk(way, -lax.div(i, 2)), part_half(way, i)

    def late_rows(spot):
        index, part = spot
        return pl.ds(pl.multiple_of((index * 2 + part) * late_width, late_width), late_width)

    def early_rows(spot, owner):
        index, part = spot
        start = ((index * 2 + owner) * 2 + part) * early_width
        return pl.ds(pl.multiple_of(start, early_width), early_width)

    def late_part(spot):
        return dot(mixed[0:cut], weight[late_rows(spot), :], NT)

    def early_part(spot, owner):
        return dot(mixed[cut:], weight[early_rows(spot, owner), :], NT)

    def remote(source, target, send, recv, device):
        return pltpu.make_async_remote_copy(
            src_ref=source,
            dst_ref=target,
            send_sem=send,
            recv_sem=recv,
            device_id=device,
            device_id_type=MESH,
        )

    def late_reduce(way, i, j):
        return remote(
            late_out.at[way, i, j],
            late_moving.at[way, i, j],
            late_reduce_send.at[way, i, j],
            late_reduce_recv.at[way, i, j],
            ways[way],
        )

    def early_reduce(way, i, j):
        return remote(
            early_out.at[way, i, j],
            early_moving.at[way, i, j],
            early_reduce_send.at[way, i, j],
            early_reduce_recv.at[way, i, j],
            ways[way],
        )

    def halve_copy(way, i, j):
        return remote(
            halve_out.at[way, i, j],
            halve_in.at[way, i, j],
            halve_send.at[way, i, j],
            halve_recv.at[way, i, j],
            across,
        )

    def swap_copy(way, j):
        return remote(
            swap_out.at[way, j], swap_in.at[way, j], swap_send.at[way, j], swap_recv.at[way, j], across
        )

    def late_gather(way, i, j):
        index, part = gather_spot(way, i)
        spot = late_hidden.at[index, part, j]
        return remote(
            spot, spot, late_gather_send.at[way, i, j], late_gather_recv.at[way, i, j], ways[way]
        )

    def early_gather(way, i, j):
        index, part = gather_spot(way, i)
        spot = early_hidden.at[index, side, part, j]
        return remote(
            spot, spot, early_gather_send.at[way, i, j], early_gather_recv.at[way, i, j], ways[way]
        )

    def arrived_spot(way, i):
        return chunk(way, -lax.div(i, 2) - 1), part_half(way, i)

    def join_copy(way, i, j, at):
        index, part = at
        spot = early_hidden.at[index, side, part, j]
        return remote(spot, spot, join_send.at[way, i, j], join_recv.at[way, i, j], across)

    late_turns = [(j, way) for j in range(late_pieces) for way in range(2)]
    early_turns = [(j, way) for j in range(early_pieces) for way in range(2)]

    def cut_piece(value, j):
        return value[j * piece : (j + 1) * piece]

    def start_halving(i, at=None):
        for way in range(2):
            part = early_part(reduce_spot(way, i) if at is None else at[way], 1 - side)
            for j in range(early_pieces):
                halve_out[way, i, j] = cut_piece(part, j).astype(jnp.bfloat16)
                halve_copy(way, i, j).start()

    def start_late(i):
        for way in range(2):
            part = late_part(reduce_spot(way, i))
            for j in range(late_pieces):
                late_out[way, i, j] = cut_piece(part, j).astype(jnp.bfloat16)
                late_reduce(way, i, j).start()

    def start_early(i):
        parts = [early_part(reduce_spot(way, i), side) for way in range(2)]
        for j, way in early_turns:
            halve_copy(way, i, j).wait_recv()
            early_out[way, i, j] = (
                cut_piece(parts[way], j) + halve_in[way, i, j].astype(jnp.float32)
            ).astype(jnp.bfloat16)
            early_reduce(way, i, j).start()

    start_halving(0)
    start_late(0)
    start_halving(1)
    start_late(1)
    start_halving(2)
    start_early(0)
    start_halving(3)
    start_early(1)

    along = dot(
        jnp.broadcast_to(reward_channels, (8, channels)), mixed[...].astype(jnp.float32), NT, HIGH
    )

    own_spots = [(place, way) for way in range(2)]

    def reduce_work(i):
        late_parts = [late_part(reduce_spot(way, i + 2)) for way in range(2)]
        early_parts = [early_part(reduce_spot(way, i + 2), side) for way in range(2)]

        def late_turn(j, way):
            late_reduce(way, i, j).wait_recv()
            late_out[way, i + 2, j] = (
                late_moving[way, i, j].astype(jnp.float32) + cut_piece(late_parts[way], j)
            ).astype(jnp.bfloat16)
            late_reduce(way, i + 2, j).start()

        def early_turn(j, way):
            halve_copy(way, i + 2, j).wait_recv()
            early_reduce(way, i, j).wait_recv()
            early_out[way, i + 2, j] = (
                early_moving[way, i, j].astype(jnp.float32)
                + cut_piece(early_parts[way], j)
                + halve_in[way, i + 2, j].astype(jnp.float32)
            ).astype(jnp.bfloat16)
            early_reduce(way, i + 2, j).start()

        for k in range(max(len(late_turns), len(early_turns))):
            if k < len(late_turns):
                late_turn(*late_turns[k])
            if k < len(early_turns):
                early_turn(*early_turns[k])

    def reduce_step(i, _):
        start_halving(i + 4)
        reduce_work(i)
        return 0

    lax.fori_loop(0, last - 3, reduce_step, 0)
    start_halving(last + 1, own_spots)
    lax.fori_loop(last - 3, last - 1, lambda i, _: reduce_work(i) or 0, 0)

    late_parts = [late_part(own_spots[way]) for way in range(2)]
    early_parts = [early_part(own_spots[way], side) for way in range(2)]
    for j, way in late_turns:
        late_reduce(1 - way, last - 1, j).wait_recv()
        late_reduce(way, last, j).wait_recv()
        swap_out[way, j] = (
            late_moving[way, last, j].astype(jnp.float32)
            + late_moving[1 - way, last - 1, j].astype(jnp.float32)
            + cut_piece(late_parts[way], j)
        ).astype(jnp.bfloat16)
        swap_copy(way, j).start()
    for j, way in early_turns:
        halve_copy(way, last + 1, j).wait_recv()
        early_reduce(1 - way, last - 1, j).wait_recv()
        early_reduce(way, last, j).wait_recv()
        early_hidden[place, side, way, j] = (
            early_moving[way, last, j].astype(jnp.float32)
            + early_moving[1 - way, last - 1, j].astype(jnp.float32)
            + cut_piece(early_parts[way], j)
            + halve_in[way, last + 1, j].astype(jnp.float32)
        ).astype(jnp.bfloat16)
        early_gather(way, 0, j).start()
        early_gather(1 - way, 1, j).start()
    for j, way in late_turns:
        swap_copy(way, j).wait_recv()
        late_hidden[place, way, j] = (
            swap_out[way, j].astype(jnp.float32) + swap_in[way, j].astype(jnp.float32)
        ).astype(jnp.bfloat16)
        late_gather(way, 0, j).start()
        late_gather(1 - way, 1, j).start()
    for j, way in early_turns:
        join_copy(way, 0, j, own_spots[way]).start()

    def squares(read, columns_count):
        total = None
        for way in range(2):
            value = read(way).astype(jnp.float32)
            total = value * value if total is None else total + value * value
        return dot(jnp.ones((8, columns_count), jnp.float32), total, NT, HIGH)

    late_squares = squares(lambda way: late_hidden[place, way].reshape(cut, late_width), late_width)
    early_squares = squares(
        lambda way: early_hidden[place, side, way].reshape(tokens - cut, early_width), early_width
    )
    is_along = iota((8, tokens), 0) == 0
    own_stats[...] = jnp.where(
        is_along, along, jnp.concatenate([0.5 * late_squares, early_squares], axis=1)
    )

    def stats_copy(k):
        return remote(
            own_stats,
            far_stats.at[k],
            stats_send.at[k],
            stats_recv.at[k],
            (seq, lax.rem(tensor + k, tensor_count)),
        )

    def reward_copy(k):
        return remote(
            own_reward,
            rewards.at[seq],
            reward_send.at[k],
            reward_recv.at[k],
            (lax.rem(seq + k, seq_count), tensor),
        )

    def start_stats(k, _):
        stats_copy(k).start()
        return 0

    lax.fori_loop(1, tensor_count, start_stats, 0)

    def late_back(spot):
        index, part = spot
        return dot(late_hidden[index, part].reshape(cut, late_width), weight[late_rows(spot), :], NN)

    def early_back(spot, owner):
        index, part = spot
        return dot(
            early_hidden[index, owner, part].reshape(tokens - cut, early_width),
            weight[early_rows(spot, owner), :],
            NN,
        )

    def add_joined(i, spots):
        for j, way in early_turns:
            join_copy(way, i, j, spots[way]).wait_recv()
        back[cut:] += early_back(spots[0], 1 - side) + early_back(spots[1], 1 - side)

    back[0:cut] = late_back(own_spots[0]) + late_back(own_spots[1])
    back[cut:] = early_back(own_spots[0], side) + early_back(own_spots[1], side)

    def take(i, forward):
        spots = [arrived_spot(way, i) for way in range(2)]
        for k in range(max(len(late_turns), len(early_turns))):
            if k < len(early_turns):
                j, way = early_turns[k]
                early_gather(way, i, j).wait_recv()
                if forward:
                    early_gather(way, i + 2, j).start()
                join_copy(way, i + 1, j, spots[way]).start()
            if k < len(late_turns):
                j, way = late_turns[k]
                late_gather(way, i, j).wait_recv()
                if forward:
                    late_gather(way, i + 2, j).start()
        back[0:cut] += late_back(spots[0]) + late_back(spots[1])
        back[cut:] += early_back(spots[0], side) + early_back(spots[1], side)

    def gather_step(i, _):
        take(i, True)
        add_joined(i, [arrived_spot(way, i - 1) for way in range(2)])
        return 0

    take(0, True)
    add_joined(0, own_spots)
    gather_step(1, 0)

    def add_stats(k, total):
        stats_copy(k).wait_recv()
        return total + far_stats[k]

    stats = lax.fori_loop(1, tensor_count, add_stats, own_stats[...])
    scale = jnp.sqrt(stats[1:2] / model_width + norm_eps)
    own_reward[...] = jnp.broadcast_to(stats[0:1] / scale, own_reward.shape)
    rewards[seq] = own_reward[...]

    def start_reward(k, _):
        reward_copy(k).start()
        return 0

    lax.fori_loop(1, seq_count, start_reward, 0)
    lax.fori_loop(2, last - 1, gather_step, 0)
    for i in (last - 1, last):
        take(i, False)
        add_joined(i, [arrived_spot(way, i - 1) for way in range(2)])
    add_joined(last + 1, [arrived_spot(way, last) for way in range(2)])

    def end_reward(k, _):
        reward_copy(k).wait()
        return 0

    lax.fori_loop(1, seq_count, end_reward, 0)

    reward_out[...] = own_reward[0:1]

    facts = jnp.concatenate(
        [stats, jnp.broadcast_to(scale, stats.shape), own_reward[...]]
        + [jnp.zeros((BLOCK - 24, tokens), jnp.float32)],
        axis=0,
    ).T
    lane = iota(tile, 1)
    for tb in range(blocks):
        mate = mate_all[span(tb)].astype(jnp.int32)
        sign = sign_all[span(tb), 0:1]

        def look(i, total):
            for k in range(blocks):
                row = rewards[i, 0:1, k * BLOCK : (k + 1) * BLOCK]
                total = total + jnp.where(mate == lane + (i * tokens + k * BLOCK), row, 0.0)
            return total

        mate_reward = jnp.sum(
            lax.fori_loop(0, seq_count, look, jnp.zeros(tile, jnp.float32)), axis=1, keepdims=True
        )
        own_along = facts[span(tb), 0:1]
        own_scale = facts[span(tb), 8:9]
        push = sign * (facts[span(tb), 16:17] - mate_reward)
        pair_grad = sign * (loss_scale / (1.0 + jnp.exp(-push)))
        y, z, sig, silu, gated, inverse = gating(tb)
        d_gained = gain * (
            (pair_grad / own_scale)
            * (reward_channels - (own_along / (model_width * own_scale * own_scale)) * back[span(tb)])
        )
        shared = jnp.sum(gated * d_gained, axis=1, keepdims=True) / channels
        d_gated = inverse * d_gained - gated * (inverse * inverse * inverse * shared)
        dz_ref[span(tb)] = (d_gated * y * (sig * (1.0 + z * (1.0 - sig)))).astype(jnp.bfloat16)
        dy = d_gated * silu
        dy_all[span(tb)] = dy.astype(jnp.bfloat16)
        faded_dy[span(tb)] = (dy * expanded(1, tb)).astype(jnp.bfloat16)
        dx_all[span(tb)] = skip * dy
        product = dy * carried_all[span(tb)]
        total = jnp.zeros(tile, jnp.float32)
        for h in range(heads):
            total = total + jnp.where(
                lane == h, jnp.sum(product[:, lanes(h)], axis=1, keepdims=True), 0.0
            )
        sums[span(tb)] = total
    grad_out[0:STATE] = dot(c_ref[...], faded_dy[...], TN).astype(jnp.bfloat16)
    grad_out[STATE:] = through_rows
    for distance in range(1, reach + 1):
        grad_copy(distance).start()

    column_sums[...] = jnp.zeros_like(column_sums)
    db_all[...] = jnp.zeros_like(db_all)
    for tb in range(blocks):
        reached = (tb + 1) * BLOCK
        score = scores[span(tb), 0:reached]
        d_score = None
        row_sums = sums[span(tb)]
        for h in range(heads):
            dy = dy_all[span(tb), lanes(h)]
            decay = decays[h, span(tb), 0:reached]
            d_decayed = decay * dot(dy, x_ref[0:reached, lanes(h)], NT)
            d_score = d_decayed if d_score is None else d_score + d_decayed
            weighed = d_decayed * score
            row_sums = row_sums + jnp.where(
                lane == h, jnp.sum(weighed, axis=1, keepdims=True), 0.0
            )
            column_sums[h : h + 1, 0:reached] += jnp.sum(weighed, axis=0, keepdims=True)
            dx_all[0:reached, lanes(h)] += dot((decay * score).astype(jnp.bfloat16), dy, TN)
        sums[span(tb)] = row_sums
        d_score = d_score.astype(jnp.bfloat16)
        maps_wide[pl.ds(2 * tb * BLOCK + 1, BLOCK, stride=2), :] = dot(
            d_score, b_ref[0:reached], NN
        ) + dot(faded_dy[span(tb)], incoming, NT)
        db_all[0:reached] += dot(d_score, c_ref[span(tb)], TN)

    for distance in range(1, reach + 1):
        grad_copy(distance).wait_recv()
    grad_end = gathered(grad_far)
    crossing = jnp.sum(grad_end * state_in[...], axis=0, keepdims=True)
    grad_end = grad_end.astype(jnp.bfloat16)
    for tb in range(blocks):
        d_weighted = expanded(0, tb) * dot(b_ref[span(tb)], grad_end, NN)
        dx_ref[span(tb)] = (dx_all[span(tb)] + d_weighted).astype(jnp.bfloat16)
        maps_wide[pl.ds(2 * tb * BLOCK, BLOCK, stride=2), :] = db_all[span(tb)] + dot(
            weighted_x[span(tb)], grad_end, NT
        )
        product = d_weighted * x_ref[span(tb)].astype(jnp.float32)
        total = sums[span(tb)]
        for h in range(heads):
            total = total + jnp.where(
                lane == h + 8, jnp.sum(product[:, lanes(h)], axis=1, keepdims=True), 0.0
            )
        sums[span(tb)] = total
    dmaps_ref[...] = maps_wide[...].astype(jnp.bfloat16)
    turned = sums[...].T
    weight_sums = turned[8:16]
    reach_end = jnp.zeros((8, 1), jnp.float32)
    for h in range(heads):
        reach_end = reach_end + jnp.where(
            iota((8, 1), 0) == h, jnp.sum(crossing[:, lanes(h)], axis=1, keepdims=True), 0.0
        )
    d_last = jnp.sum(weight_sums, axis=1, keepdims=True) + through * reach_end
    d_cumulative = turned[0:8] - column_sums[...] - weight_sums
    d_cumulative = d_cumulative + jnp.where(iota(step.shape, 1) == tokens - 1, d_last, 0.0)
    onward = (iota(square, 0) >= iota(square, 1)).astype(jnp.float32)
    d_exponent = dot(d_cumulative, onward, NN, HIGH)
    d_step = (column_sums[...] + weight_sums) / step - rate * d_exponent
    dstep_ref[...] = (d_step / (1.0 + jnp.exp(-pre)))[0:heads]

    for distance in range(1, reach + 1):
        state_copy(distance).wait_send()
        grad_copy(distance).wait_send()

    def end_stats(k, _):
        stats_copy(k).wait_send()
        return 0

    lax.fori_loop(1, tensor_count, end_stats, 0)

    def end_ring(step, _):
        for j, way in late_turns:
            late_reduce(way, step, j).wait_send()
            late_gather(way, step, j).wait_send()
        for j, way in early_turns:
            early_reduce(way, step, j).wait_send()
            early_gather(way, step, j).wait_send()
        return 0

    def end_side(step, _):
        for j, way in early_turns:
            halve_copy(way, step, j).wait_send()
            join_copy(way, step, j, own_spots[way]).wait_send()
        return 0

    lax.fori_loop(0, chips - 1, end_ring, 0)
    lax.fori_loop(0, chips, end_side, 0)
    for j, way in late_turns:
        swap_copy(way, j).wait_send()


def deliver_kernel(*refs):
    count = len(refs) // 2
    for source, target in zip(refs[:count], refs[count:]):
        target[...] = source[...]


def deliver(values):
    vmem = pl.BlockSpec(memory_space=pltpu.VMEM)
    return pl.pallas_call(
        deliver_kernel,
        out_shape=tuple(jax.ShapeDtypeStruct(v.shape, v.dtype) for v in values),
        in_specs=[vmem] * len(values),
        out_specs=(vmem,) * len(values),
        compiler_params=pltpu.CompilerParams(vmem_limit_bytes=60 << 20),
        name="deliver",
    )(*values)


def on_device(
    ssd_input,
    gate_input,
    state_maps,
    step_raw,
    step_bias,
    decay_rate,
    skip_gain,
    norm_gain,
    out_weight,
    reward_head,
    traj_lengths,
    step_pairs,
):
    tokens, channels = ssd_input.shape
    heads = step_raw.shape[1]
    model_width = out_weight.shape[0]
    seq_count, tensor_count = lax.axis_size("seq"), lax.axis_size("tensor")
    chips = tensor_count // 2
    late_width = model_width // (2 * chips)
    early_width = late_width // 2
    late_pieces, early_pieces = 1, 1
    piece = tokens // (late_pieces + early_pieces)
    steps = chips - 1
    reach = -(-(longest - 1) // tokens)
    bf16, f32 = jnp.bfloat16, jnp.float32

    operands = (
        ssd_input,
        gate_input,
        state_maps.reshape(2 * tokens, STATE),
        step_raw.T,
        step_bias,
        decay_rate,
        skip_gain,
        norm_gain[None, :],
        out_weight,
        reward_head[None, :],
        traj_lengths[None, :],
        step_pairs[None, :],
    )
    vmem = pl.BlockSpec(memory_space=pltpu.VMEM)
    hbm = pl.BlockSpec(memory_space=pltpu.HBM)
    smem = pl.BlockSpec(memory_space=pltpu.SMEM)
    results = pl.pallas_call(
        layer_kernel,
        out_shape=(
            jax.ShapeDtypeStruct((1, tokens), f32),
            jax.ShapeDtypeStruct((tokens, channels), bf16),
            jax.ShapeDtypeStruct((tokens, channels), bf16),
            jax.ShapeDtypeStruct((2 * tokens, STATE), bf16),
            jax.ShapeDtypeStruct((heads, tokens), f32),
        ),
        in_specs=[hbm] * 4 + [smem] * 3 + [hbm] * 5,
        out_specs=(vmem,) * 5,
        scratch_shapes=[
            pltpu.VMEM((model_width, channels), bf16),
            pltpu.VMEM((tokens, channels), bf16),
            pltpu.VMEM((tokens, channels), bf16),
            pltpu.VMEM((2 * tokens, STATE), bf16),
            pltpu.VMEM((heads, tokens), f32),
            pltpu.VMEM((1, channels), f32),
            pltpu.VMEM((1, model_width), f32),
            pltpu.VMEM((1, traj_lengths.shape[0]), jnp.int32),
            pltpu.VMEM((1, step_pairs.shape[0]), jnp.int32),
            pltpu.VMEM((2 * tokens, STATE), f32),
            pltpu.VMEM((tokens, STATE), bf16),
            pltpu.VMEM((tokens, STATE), bf16),
            pltpu.VMEM((tokens, BLOCK), f32),
            pltpu.VMEM((heads, tokens, tokens), f32),
            pltpu.VMEM((tokens, tokens), f32),
            pltpu.VMEM((tokens, channels), f32),
            pltpu.VMEM((tokens, channels), f32),
            pltpu.VMEM((STATE, channels), f32),
            pltpu.VMEM((tokens, channels), bf16),
            pltpu.VMEM((tokens, channels), bf16),
            pltpu.VMEM((tokens, BLOCK), f32),
            pltpu.VMEM((tokens, BLOCK), f32),
            pltpu.VMEM((STATE + 16, channels), bf16),
            pltpu.VMEM((reach, STATE + 16, channels), bf16),
            pltpu.VMEM((STATE + 16, channels), bf16),
            pltpu.VMEM((reach, STATE + 16, channels), bf16),
            pltpu.VMEM((tokens, channels), bf16),
            pltpu.VMEM((tokens, channels), bf16),
            pltpu.VMEM((tokens, channels), f32),
            pltpu.VMEM((tokens, STATE), f32),
            pltpu.VMEM((tokens, BLOCK), f32),
            pltpu.VMEM((8, tokens), f32),
            pltpu.VMEM((tokens, channels), f32),
            pltpu.VMEM((seq_count, 8, tokens), f32),
            pltpu.VMEM((2, steps, late_pieces, piece, late_width), bf16),
            pltpu.VMEM((2, steps, late_pieces, piece, late_width), bf16),
            pltpu.VMEM((2, late_pieces, piece, late_width), bf16),
            pltpu.VMEM((2, late_pieces, piece, late_width), bf16),
            pltpu.VMEM((chips, 2, late_pieces, piece, late_width), bf16),
            pltpu.VMEM((2, steps, early_pieces, piece, early_width), bf16),
            pltpu.VMEM((2, steps, early_pieces, piece, early_width), bf16),
            pltpu.VMEM((2, chips, early_pieces, piece, early_width), bf16),
            pltpu.VMEM((2, chips, early_pieces, piece, early_width), bf16),
            pltpu.VMEM((chips, 2, 2, early_pieces, piece, early_width), bf16),
            pltpu.VMEM((8, tokens), f32),
            pltpu.VMEM((tensor_count, 8, tokens), f32),
            pltpu.VMEM((8, tokens), f32),
            pltpu.SemaphoreType.DMA((9,)),
            pltpu.SemaphoreType.DMA((reach,)),
            pltpu.SemaphoreType.DMA((reach,)),
            pltpu.SemaphoreType.DMA((reach,)),
            pltpu.SemaphoreType.DMA((reach,)),
            pltpu.SemaphoreType.DMA((2, steps, late_pieces)),
            pltpu.SemaphoreType.DMA((2, steps, late_pieces)),
            pltpu.SemaphoreType.DMA((2, late_pieces)),
            pltpu.SemaphoreType.DMA((2, late_pieces)),
            pltpu.SemaphoreType.DMA((2, steps, late_pieces)),
            pltpu.SemaphoreType.DMA((2, steps, late_pieces)),
            pltpu.SemaphoreType.DMA((2, steps, early_pieces)),
            pltpu.SemaphoreType.DMA((2, steps, early_pieces)),
            pltpu.SemaphoreType.DMA((2, steps, early_pieces)),
            pltpu.SemaphoreType.DMA((2, steps, early_pieces)),
            pltpu.SemaphoreType.DMA((2, chips, early_pieces)),
            pltpu.SemaphoreType.DMA((2, chips, early_pieces)),
            pltpu.SemaphoreType.DMA((2, chips, early_pieces)),
            pltpu.SemaphoreType.DMA((2, chips, early_pieces)),
            pltpu.SemaphoreType.DMA((tensor_count,)),
            pltpu.SemaphoreType.DMA((tensor_count,)),
            pltpu.SemaphoreType.DMA((seq_count,)),
            pltpu.SemaphoreType.DMA((seq_count,)),
        ],
        compiler_params=pltpu.CompilerParams(
            collective_id=0, has_side_effects=True, vmem_limit_bytes=60 << 20
        ),
        name="layer",
    )(*operands)
    rewards, dx, dz, dmaps, dstep = deliver(results)
    return (
        rewards.reshape(tokens),
        dx,
        dz,
        dmaps.reshape(tokens, 2, STATE),
        dstep.T,
    )


def solution(mesh):
    return jax.shard_map(
        on_device,
        mesh=mesh,
        in_specs=(
            P("seq", "tensor"),
            P("seq", "tensor"),
            P("seq", None, "tensor"),
            P("seq", "tensor"),
            P("tensor"),
            P("tensor"),
            P("tensor"),
            P("tensor"),
            P(None, "tensor"),
            P(),
            P(),
            P(),
        ),
        out_specs=(
            P("seq"),
            P("seq", "tensor"),
            P("seq", "tensor"),
            P("seq", None, "tensor"),
            P("seq", "tensor"),
        ),
        check_vma=False,
    )
```

```python
import jax
import jax.numpy as jnp
from jax import lax
from jax.experimental import pallas as pl
from jax.experimental.pallas import tpu as pltpu
from jax.sharding import PartitionSpec as P

STATE = 128
BLOCK = 128

norm_eps = 1e-05
loss_scale = 64.0
longest = 1152
MESH = pl.DeviceIdType.MESH
HIGH = lax.Precision.HIGHEST
NT = ((1,), (1,))
NN = ((1,), (0,))
TN = ((0,), (0,))


def dot(left, right, dims, precision=None):
    return lax.dot_general(
        left, right, (dims, ((), ())), preferred_element_type=jnp.float32, precision=precision
    )


def iota(shape, axis):
    return lax.broadcasted_iota(jnp.int32, shape, axis)


def layer_kernel(
    x_hbm,
    z_hbm,
    maps_hbm,
    raw_hbm,
    bias_ref,
    rate_ref,
    skip_ref,
    gain_hbm,
    weight_hbm,
    head_hbm,
    length_hbm,
    pairs_hbm,
    reward_out,
    dx_ref,
    dz_ref,
    dmaps_ref,
    dstep_ref,
    weight,
    x_ref,
    z_ref,
    maps_ref,
    raw_ref,
    gain_ref,
    head_ref,
    length_ref,
    pairs_ref,
    maps_wide,
    b_ref,
    c_ref,
    columns,
    decays,
    scores,
    y_all,
    carried_all,
    state_in,
    mixed,
    weighted_x,
    mate_all,
    sign_all,
    state_out,
    state_far,
    grad_out,
    grad_far,
    dy_all,
    faded_dy,
    dx_all,
    db_all,
    sums,
    column_sums,
    back,
    rewards,
    late_out,
    late_moving,
    swap_out,
    swap_in,
    late_hidden,
    early_out,
    early_moving,
    halve_out,
    halve_in,
    early_hidden,
    own_stats,
    far_stats,
    own_reward,
    state_relay_out,
    state_relay_in,
    grad_relay_out,
    grad_relay_in,
    grad_in,
    kept,
    facts,
    factors,
    load_sems,
    relay_send,
    relay_recv,
    state_send,
    state_recv,
    grad_send,
    grad_recv,
    late_reduce_send,
    late_reduce_recv,
    swap_send,
    swap_recv,
    late_gather_send,
    late_gather_recv,
    early_reduce_send,
    early_reduce_recv,
    early_gather_send,
    early_gather_recv,
    halve_send,
    halve_recv,
    join_send,
    join_recv,
    stats_send,
    stats_recv,
    reward_send,
    reward_recv,
):
    seq, tensor = lax.axis_index("seq"), lax.axis_index("tensor")
    seq_count, tensor_count = lax.axis_size("seq"), lax.axis_size("tensor")
    chips = tensor_count // 2
    place, side = lax.rem(tensor, chips), tensor // chips
    base = side * chips
    up = (seq, base + lax.rem(place + 1, chips))
    down = (seq, base + lax.rem(place + chips - 1, chips))
    across = (seq, (1 - side) * chips + place)
    ways = (up, down)
    tokens, channels = x_ref.shape
    model_width = weight.shape[0]
    late_pieces, piece, late_width = late_hidden.shape[2:]
    early_pieces, _, early_width = early_hidden.shape[3:]
    cut = late_pieces * piece
    width = channels // (raw_ref.shape[0])
    heads = channels // width
    blocks = tokens // BLOCK
    reach = state_far.shape[0]
    pair_tiles = pairs_ref.shape[1] // BLOCK

    loads = [
        pltpu.make_async_copy(source, target, load_sems.at[k])
        for k, (source, target) in enumerate(
            [
                (raw_hbm, raw_ref),
                (length_hbm, length_ref),
                (maps_hbm, maps_ref),
                (x_hbm, x_ref),
                (pairs_hbm, pairs_ref),
                (head_hbm, head_ref),
                (gain_hbm, gain_ref),
                (z_hbm, z_ref),
                (weight_hbm, weight),
            ]
        )
    ]
    for load in loads:
        load.start()
    barrier = pltpu.get_barrier_semaphore()

    def greet_tensor(k, _):
        other = lax.rem(tensor + k, tensor_count)
        pl.semaphore_signal(barrier, inc=1, device_id=(seq, other), device_id_type=MESH)
        return 0

    def greet_seq(k, _):
        other = lax.rem(seq + k, seq_count)
        pl.semaphore_signal(barrier, inc=1, device_id=(other, tensor), device_id_type=MESH)
        return 0

    lax.fori_loop(1, tensor_count, greet_tensor, 0)
    lax.fori_loop(1, seq_count, greet_seq, 0)

    def span(tb):
        return slice(tb * BLOCK, (tb + 1) * BLOCK)

    def lanes(h):
        return slice(h * width, (h + 1) * width)

    def per_head(ref):
        row = lax.rem(iota((8, 1), 0), heads)
        return sum(jnp.where(row == h, ref[h], 0.0) for h in range(heads))

    bias, rate = per_head(bias_ref), per_head(rate_ref)
    for load in loads[:2]:
        load.wait()
    pre = jnp.concatenate([raw_ref[...], raw_ref[...]], axis=0) + bias
    step = jnp.maximum(pre, 0.0) + jnp.log1p(jnp.exp(-jnp.abs(pre)))
    exponent = -step * rate
    square = (tokens, tokens)
    upto = (iota(square, 0) <= iota(square, 1)).astype(jnp.float32)
    cumulative = dot(exponent, upto, NN, HIGH)
    count = length_ref.shape[1]
    openings = jnp.sum(
        jnp.where(
            iota((count, count), 1) < iota((count, count), 0),
            length_ref[...].astype(jnp.float32),
            0.0,
        ),
        axis=1,
        keepdims=True,
    )
    position = (iota((count, tokens), 1) + seq * tokens).astype(jnp.float32)
    block_start = (iota((count, tokens), 0) * 0 + seq * tokens).astype(jnp.float32)
    segment = jnp.sum(
        jnp.where((openings <= position) & (openings >= block_start), 1.0, 0.0),
        axis=0,
        keepdims=True,
    )
    last_segment = segment[:, tokens - 1 :]
    last_cumulative = cumulative[:, tokens - 1 :]
    end_weight = jnp.where(
        jnp.broadcast_to(segment == last_segment, step.shape),
        jnp.exp(last_cumulative - cumulative),
        0.0,
    )
    end_weight = end_weight * step
    first_weight = jnp.where(
        jnp.broadcast_to(segment == 0.0, step.shape), jnp.exp(cumulative), 0.0
    )
    through = jnp.where(last_segment == 0.0, jnp.exp(last_cumulative), 0.0)
    segment_rows = jnp.broadcast_to(segment, step.shape)
    columns[...] = jnp.concatenate(
        [
            end_weight,
            first_weight,
            cumulative,
            segment_rows,
            jnp.zeros((BLOCK - 32, tokens), jnp.float32),
        ],
        axis=0,
    ).T

    def column(kind, h, tb):
        return columns[span(tb), kind * 8 + h : kind * 8 + h + 1]

    def expanded(kind, tb):
        return jnp.concatenate(
            [jnp.broadcast_to(column(kind, h, tb), (BLOCK, width)) for h in range(heads)], axis=1
        )

    through_wide = jnp.concatenate(
        [jnp.broadcast_to(through[h : h + 1], (1, width)) for h in range(heads)], axis=1
    )
    through_high = through_wide.astype(jnp.bfloat16).astype(jnp.float32)
    tail_shape = (16, channels)
    through_rows = jnp.where(
        iota(tail_shape, 0) == 0,
        through_high,
        jnp.where(iota(tail_shape, 0) == 1, through_wide - through_high, 0.0),
    ).astype(jnp.bfloat16)

    def far_copy(source, target, send, recv, distance, direction):
        return pltpu.make_async_remote_copy(
            src_ref=source,
            dst_ref=target.at[distance - 1],
            send_sem=send.at[distance - 1],
            recv_sem=recv.at[distance - 1],
            device_id=(lax.rem(seq + seq_count + direction * distance, seq_count), tensor),
            device_id_type=MESH,
        )

    def state_copy(distance):
        return far_copy(state_out, state_far, state_send, state_recv, distance, 1)

    def grad_copy(distance):
        return far_copy(grad_out, grad_far, grad_send, grad_recv, distance, -1)

    def relay_copy(buffer_out, buffer_in, send, recv, direction):
        return pltpu.make_async_remote_copy(
            src_ref=buffer_out,
            dst_ref=buffer_in,
            send_sem=send,
            recv_sem=recv,
            device_id=(lax.rem(seq + seq_count + direction, seq_count), tensor),
            device_id_type=MESH,
        )

    def state_relay():
        return relay_copy(state_relay_out, state_relay_in, relay_send.at[0], relay_recv.at[0], 1)

    def grad_relay():
        return relay_copy(grad_relay_out, grad_relay_in, relay_send.at[1], relay_recv.at[1], -1)

    parity = lax.rem(seq, 2)

    def for_parity(taker, copy, direction, act):
        for kind in range(2):

            @pl.when(parity == kind)
            def _():
                for distance in range(1, reach + 1):
                    if (kind + direction * distance) % 2 == taker:
                        act(copy(distance))

    def gathered(far):
        total, carry = None, None
        for k in range(reach):
            value = far[k, 0:STATE].astype(jnp.float32)
            passed = far[k, STATE : STATE + 1].astype(jnp.float32) + far[
                k, STATE + 1 : STATE + 2
            ].astype(jnp.float32)
            if total is None:
                total, carry = value, passed
            else:
                total = total + carry * value
                carry = carry * passed
        return total

    loads[2].wait()
    maps_wide[...] = maps_ref[...].astype(jnp.float32)
    b_ref[...] = maps_wide[pl.ds(0, tokens, stride=2), :].astype(jnp.bfloat16)
    c_ref[...] = maps_wide[pl.ds(1, tokens, stride=2), :].astype(jnp.bfloat16)
    loads[3].wait()
    for tb in range(blocks):
        weighted_x[span(tb)] = (
            x_ref[span(tb)].astype(jnp.float32) * expanded(0, tb)
        ).astype(jnp.bfloat16)
    state_out[0:STATE] = dot(b_ref[...], weighted_x[...], TN).astype(jnp.bfloat16)
    state_out[STATE:] = through_rows
    pl.semaphore_wait(barrier, tensor_count + seq_count - 2)
    for_parity(0, state_copy, 1, lambda copy: copy.start())

    for tb in range(blocks):
        reached = (tb + 1) * BLOCK
        score = dot(c_ref[span(tb)], b_ref[0:reached], NT)
        scores[span(tb), 0:reached] = score
        shape = (BLOCK, reached)
        allowed = (column(3, 0, tb) == segment[:, 0:reached]) & (
            iota(shape, 1) <= iota(shape, 0) + tb * BLOCK
        )
        for h in range(heads):
            spread = column(2, h, tb) - cumulative[h : h + 1, 0:reached]
            decay = jnp.exp(jnp.where(allowed, spread, -1e30)) * step[h : h + 1, 0:reached]
            decays[h, span(tb), 0:reached] = decay
            y_all[span(tb), lanes(h)] = dot(
                (decay * score).astype(jnp.bfloat16), x_ref[0:reached, lanes(h)], NN
            )

    for load in loads[4:8]:
        load.wait()
    reward_row = head_ref[...]
    high = reward_row.astype(jnp.bfloat16).astype(jnp.float32)
    rest = reward_row - high
    middle = rest.astype(jnp.bfloat16).astype(jnp.float32)
    term = iota((8, model_width), 0)
    terms = jnp.where(
        term == 0,
        high,
        jnp.where(term == 1, middle, jnp.where(term == 2, rest - middle, 0.0)),
    ).astype(jnp.bfloat16)
    loads[8].wait()
    reward_channels = jnp.sum(dot(terms, weight[...], NN), axis=0, keepdims=True)

    @pl.when(parity == 0)
    def _():
        for distance in range(1, reach + 1):
            state_copy(distance).wait_recv()
        total = gathered(state_far)
        state_in[...] = total
        state_relay_out[...] = (
            state_out[0:STATE].astype(jnp.float32) + through_wide * total
        ).astype(jnp.bfloat16)
        state_relay().start()

    @pl.when(parity == 1)
    def _():
        state_relay().wait_recv()
        state_in[...] = state_relay_in[...].astype(jnp.float32)

    incoming = state_in[...].astype(jnp.bfloat16)
    gain = gain_ref[...]
    skip = jnp.concatenate([jnp.full((1, width), skip_ref[h]) for h in range(heads)], axis=1)

    def gating(tb):
        y = y_all[span(tb)]
        z = z_ref[span(tb)].astype(jnp.float32)
        sig = 1.0 / (1.0 + jnp.exp(-z))
        silu = z * sig
        gated = y * silu
        mean_square = jnp.sum(gated * gated, axis=1, keepdims=True) / channels
        return y, z, sig, silu, gated, lax.rsqrt(mean_square + norm_eps)

    for tb in range(blocks):
        carried = expanded(1, tb) * dot(c_ref[span(tb)], incoming, NN)
        carried_all[span(tb)] = carried
        y_all[span(tb)] = (
            y_all[span(tb)] + carried + skip * x_ref[span(tb)].astype(jnp.float32)
        )
        _, _, _, _, gated, inverse = gating(tb)
        mixed[span(tb)] = (gated * inverse * gain).astype(jnp.bfloat16)

    tile = (BLOCK, BLOCK)
    unroll = 4
    def search(tb):
        token = iota(tile, 0) + (seq * tokens + tb * BLOCK)

        def find(i, total):
            for k in range(unroll):
                start = pl.multiple_of((i * unroll + k) * BLOCK, BLOCK)
                row = pairs_ref[0:1, pl.ds(start, BLOCK)]
                order = (iota(tile, 1) + start).astype(jnp.float32)
                total = total + jnp.where(row == token, order, 0.0)
            return total

        zero = jnp.zeros(tile, jnp.float32)
        order = jnp.sum(
            lax.fori_loop(0, pair_tiles // unroll, find, zero), axis=1, keepdims=True
        )
        odd = order - 2.0 * jnp.floor(order * 0.5)
        other = jnp.broadcast_to(order + 1.0 - 2.0 * odd, tile)

        def fetch(i, total):
            for k in range(unroll):
                start = pl.multiple_of((i * unroll + k) * BLOCK, BLOCK)
                row = pairs_ref[0:1, pl.ds(start, BLOCK)].astype(jnp.float32)
                order = (iota(tile, 1) + start).astype(jnp.float32)
                total = total + jnp.where(other == order, row, 0.0)
            return total

        mate = jnp.sum(
            lax.fori_loop(0, pair_tiles // unroll, fetch, zero), axis=1, keepdims=True
        )
        mate_all[span(tb)] = jnp.broadcast_to(mate, tile)
        sign_all[span(tb)] = jnp.broadcast_to(2.0 * odd - 1.0, tile)

    last = chips - 2

    def chunk(way, distance):
        return lax.rem(place + chips + (distance if way == 0 else -distance), chips)

    def part_half(way, i):
        odd = lax.rem(i, 2)
        return odd if way == 0 else 1 - odd

    def reduce_spot(way, i):
        return chunk(way, chips // 2 - lax.div(i + 1, 2)), part_half(way, i)

    def gather_spot(way, i):
        return chunk(way, -lax.div(i, 2)), part_half(way, i)

    def late_rows(spot):
        index, part = spot
        return pl.ds(pl.multiple_of((index * 2 + part) * late_width, late_width), late_width)

    def early_rows(spot, owner):
        index, part = spot
        start = ((index * 2 + owner) * 2 + part) * early_width
        return pl.ds(pl.multiple_of(start, early_width), early_width)

    def late_part(spot):
        return dot(mixed[0:cut], weight[late_rows(spot), :], NT)

    def early_part(spot, owner):
        return dot(mixed[cut:], weight[early_rows(spot, owner), :], NT)

    def remote(source, target, send, recv, device):
        return pltpu.make_async_remote_copy(
            src_ref=source,
            dst_ref=target,
            send_sem=send,
            recv_sem=recv,
            device_id=device,
            device_id_type=MESH,
        )

    def late_reduce(way, i, j):
        return remote(
            late_out.at[way, i, j],
            late_moving.at[way, i, j],
            late_reduce_send.at[way, i, j],
            late_reduce_recv.at[way, i, j],
            ways[way],
        )

    def early_reduce(way, i, j):
        return remote(
            early_out.at[way, i, j],
            early_moving.at[way, i, j],
            early_reduce_send.at[way, i, j],
            early_reduce_recv.at[way, i, j],
            ways[way],
        )

    def halve_copy(way, i, j):
        return remote(
            halve_out.at[way, i, j],
            halve_in.at[way, i, j],
            halve_send.at[way, i, j],
            halve_recv.at[way, i, j],
            across,
        )

    def swap_copy(way, j):
        return remote(
            swap_out.at[way, j], swap_in.at[way, j], swap_send.at[way, j], swap_recv.at[way, j], across
        )

    def late_gather(way, i, j):
        index, part = gather_spot(way, i)
        spot = late_hidden.at[index, part, j]
        return remote(
            spot, spot, late_gather_send.at[way, i, j], late_gather_recv.at[way, i, j], ways[way]
        )

    def early_gather(way, i, j):
        index, part = gather_spot(way, i)
        spot = early_hidden.at[index, side, part, j]
        return remote(
            spot, spot, early_gather_send.at[way, i, j], early_gather_recv.at[way, i, j], ways[way]
        )

    def arrived_spot(way, i):
        return chunk(way, -lax.div(i, 2) - 1), part_half(way, i)

    def join_copy(way, i, j, at):
        index, part = at
        spot = early_hidden.at[index, side, part, j]
        return remote(spot, spot, join_send.at[way, i, j], join_recv.at[way, i, j], across)

    late_turns = [(j, way) for j in range(late_pieces) for way in range(2)]
    early_turns = [(j, way) for j in range(early_pieces) for way in range(2)]

    def cut_piece(value, j):
        return value[j * piece : (j + 1) * piece]

    def start_halving(i, at=None):
        for way in range(2):
            part = early_part(reduce_spot(way, i) if at is None else at[way], 1 - side)
            for j in range(early_pieces):
                halve_out[way, i, j] = cut_piece(part, j).astype(jnp.bfloat16)
                halve_copy(way, i, j).start()

    def start_late(i):
        for way in range(2):
            part = late_part(reduce_spot(way, i))
            for j in range(late_pieces):
                late_out[way, i, j] = cut_piece(part, j).astype(jnp.bfloat16)
                late_reduce(way, i, j).start()

    def start_early(i):
        parts = [early_part(reduce_spot(way, i), side) for way in range(2)]
        for j, way in early_turns:
            halve_copy(way, i, j).wait_recv()
            early_out[way, i, j] = (
                cut_piece(parts[way], j) + halve_in[way, i, j].astype(jnp.float32)
            ).astype(jnp.bfloat16)
            early_reduce(way, i, j).start()

    start_halving(0)
    start_late(0)
    start_halving(1)
    start_late(1)
    start_halving(2)
    start_early(0)
    start_halving(3)
    start_early(1)

    along = dot(
        jnp.broadcast_to(reward_channels, (8, channels)), mixed[...].astype(jnp.float32), NT, HIGH
    )

    own_spots = [(place, way) for way in range(2)]

    def reduce_work(i):
        late_parts = [late_part(reduce_spot(way, i + 2)) for way in range(2)]
        early_parts = [early_part(reduce_spot(way, i + 2), side) for way in range(2)]

        def late_turn(j, way):
            late_reduce(way, i, j).wait_recv()
            late_out[way, i + 2, j] = (
                late_moving[way, i, j].astype(jnp.float32) + cut_piece(late_parts[way], j)
            ).astype(jnp.bfloat16)
            late_reduce(way, i + 2, j).start()

        def early_turn(j, way):
            halve_copy(way, i + 2, j).wait_recv()
            early_reduce(way, i, j).wait_recv()
            early_out[way, i + 2, j] = (
                early_moving[way, i, j].astype(jnp.float32)
                + cut_piece(early_parts[way], j)
                + halve_in[way, i + 2, j].astype(jnp.float32)
            ).astype(jnp.bfloat16)
            early_reduce(way, i + 2, j).start()

        for k in range(max(len(late_turns), len(early_turns))):
            if k < len(late_turns):
                late_turn(*late_turns[k])
            if k < len(early_turns):
                early_turn(*early_turns[k])

    def reduce_step(i, _):
        start_halving(i + 4)
        reduce_work(i)
        return 0

    for tb in range(blocks):
        reduce_step(tb, 0)
        search(tb)
    start_halving(last + 1, own_spots)
    lax.fori_loop(last - 3, last - 1, lambda i, _: reduce_work(i) or 0, 0)

    late_parts = [late_part(own_spots[way]) for way in range(2)]
    early_parts = [early_part(own_spots[way], side) for way in range(2)]
    for j, way in late_turns:
        late_reduce(1 - way, last - 1, j).wait_recv()
        late_reduce(way, last, j).wait_recv()
        swap_out[way, j] = (
            late_moving[way, last, j].astype(jnp.float32)
            + late_moving[1 - way, last - 1, j].astype(jnp.float32)
            + cut_piece(late_parts[way], j)
        ).astype(jnp.bfloat16)
        swap_copy(way, j).start()
    for j, way in early_turns:
        halve_copy(way, last + 1, j).wait_recv()
        early_reduce(1 - way, last - 1, j).wait_recv()
        early_reduce(way, last, j).wait_recv()
        early_hidden[place, side, way, j] = (
            early_moving[way, last, j].astype(jnp.float32)
            + early_moving[1 - way, last - 1, j].astype(jnp.float32)
            + cut_piece(early_parts[way], j)
            + halve_in[way, last + 1, j].astype(jnp.float32)
        ).astype(jnp.bfloat16)
        early_gather(way, 0, j).start()
        early_gather(1 - way, 1, j).start()
    for j, way in late_turns:
        swap_copy(way, j).wait_recv()
        late_hidden[place, way, j] = (
            swap_out[way, j].astype(jnp.float32) + swap_in[way, j].astype(jnp.float32)
        ).astype(jnp.bfloat16)
        late_gather(way, 0, j).start()
        late_gather(1 - way, 1, j).start()
    for j, way in early_turns:
        join_copy(way, 0, j, own_spots[way]).start()

    def squares(read, columns_count):
        total = None
        for way in range(2):
            value = read(way).astype(jnp.float32)
            total = value * value if total is None else total + value * value
        return dot(jnp.ones((8, columns_count), jnp.float32), total, NT, HIGH)

    late_squares = squares(lambda way: late_hidden[place, way].reshape(cut, late_width), late_width)
    early_squares = squares(
        lambda way: early_hidden[place, side, way].reshape(tokens - cut, early_width), early_width
    )
    is_along = iota((8, tokens), 0) == 0
    own_stats[...] = jnp.where(
        is_along, along, jnp.concatenate([0.5 * late_squares, early_squares], axis=1)
    )

    def stats_copy(k):
        return remote(
            own_stats,
            far_stats.at[k],
            stats_send.at[k],
            stats_recv.at[k],
            (seq, lax.rem(tensor + k, tensor_count)),
        )

    def reward_copy(k):
        return remote(
            own_reward,
            rewards.at[seq],
            reward_send.at[k],
            reward_recv.at[k],
            (lax.rem(seq + k, seq_count), tensor),
        )

    def start_stats(k, _):
        stats_copy(k).start()
        return 0

    lax.fori_loop(1, tensor_count, start_stats, 0)

    def late_back(spot):
        index, part = spot
        return dot(late_hidden[index, part].reshape(cut, late_width), weight[late_rows(spot), :], NN)

    def early_back(spot, owner):
        index, part = spot
        return dot(
            early_hidden[index, owner, part].reshape(tokens - cut, early_width),
            weight[early_rows(spot, owner), :],
            NN,
        )

    def add_joined(i, spots):
        for j, way in early_turns:
            join_copy(way, i, j, spots[way]).wait_recv()
        back[cut:] += early_back(spots[0], 1 - side) + early_back(spots[1], 1 - side)

    back[0:cut] = late_back(own_spots[0]) + late_back(own_spots[1])
    back[cut:] = early_back(own_spots[0], side) + early_back(own_spots[1], side)

    def take(i, forward):
        spots = [arrived_spot(way, i) for way in range(2)]
        for k in range(max(len(late_turns), len(early_turns))):
            if k < len(early_turns):
                j, way = early_turns[k]
                early_gather(way, i, j).wait_recv()
                if forward:
                    early_gather(way, i + 2, j).start()
                join_copy(way, i + 1, j, spots[way]).start()
            if k < len(late_turns):
                j, way = late_turns[k]
                late_gather(way, i, j).wait_recv()
                if forward:
                    late_gather(way, i + 2, j).start()
        back[0:cut] += late_back(spots[0]) + late_back(spots[1])
        back[cut:] += early_back(spots[0], side) + early_back(spots[1], side)

    def gather_step(i, _):
        take(i, True)
        add_joined(i, [arrived_spot(way, i - 1) for way in range(2)])
        return 0

    take(0, True)
    add_joined(0, own_spots)
    gather_step(1, 0)

    def add_stats(k, total):
        stats_copy(k).wait_recv()
        return total + far_stats[k]

    stats = lax.fori_loop(1, tensor_count, add_stats, own_stats[...])
    scale = jnp.sqrt(stats[1:2] / model_width + norm_eps)
    own_reward[...] = jnp.broadcast_to(stats[0:1] / scale, own_reward.shape)
    rewards[seq] = own_reward[...]

    facts[...] = jnp.concatenate(
        [stats, jnp.broadcast_to(scale, stats.shape), own_reward[...]]
        + [jnp.zeros((BLOCK - 24, tokens), jnp.float32)],
        axis=0,
    ).T
    lane = iota(tile, 1)

    def match(tb):
        mate = mate_all[span(tb)].astype(jnp.int32)
        sign = sign_all[span(tb), 0:1]

        def look(i, total):
            for k in range(blocks):
                row = rewards[i, 0:1, k * BLOCK : (k + 1) * BLOCK]
                total = total + jnp.where(mate == lane + (i * tokens + k * BLOCK), row, 0.0)
            return total

        mate_reward = jnp.sum(
            lax.fori_loop(0, seq_count, look, jnp.zeros(tile, jnp.float32)), axis=1, keepdims=True
        )
        own_along = facts[span(tb), 0:1]
        own_scale = facts[span(tb), 8:9]
        push = sign * (facts[span(tb), 16:17] - mate_reward)
        pair_grad = sign * (loss_scale / (1.0 + jnp.exp(-push)))
        hidden_factor = own_along / (model_width * own_scale * own_scale)
        factors[span(tb)] = jnp.where(lane == 0, pair_grad / own_scale, hidden_factor)

    def start_reward(k, _):
        reward_copy(k).start()
        return 0

    lax.fori_loop(1, seq_count, start_reward, 0)
    lax.fori_loop(2, last - 2, gather_step, 0)

    def end_reward(k, _):
        reward_copy(k).wait()
        return 0

    lax.fori_loop(1, seq_count, end_reward, 0)
    match(0)
    gather_step(last - 2, 0)
    for i in (last - 1, last):
        match(i - last + 2)
        take(i, False)
        add_joined(i, [arrived_spot(way, i - 1) for way in range(2)])
    add_joined(last + 1, [arrived_spot(way, last) for way in range(2)])


    reward_out[...] = own_reward[0:1]

    for tb in range(blocks):
        own_factor, hidden_factor = factors[span(tb), 0:1], factors[span(tb), 1:2]
        y, z, sig, silu, gated, inverse = gating(tb)
        d_gained = gain * (
            own_factor * (reward_channels - hidden_factor * back[span(tb)])
        )
        shared = jnp.sum(gated * d_gained, axis=1, keepdims=True) / channels
        d_gated = inverse * d_gained - gated * (inverse * inverse * inverse * shared)
        kept[span(tb)] = d_gated
        dy = d_gated * silu
        dy_all[span(tb)] = dy.astype(jnp.bfloat16)
        faded_dy[span(tb)] = (dy * expanded(1, tb)).astype(jnp.bfloat16)
    grad_out[0:STATE] = dot(c_ref[...], faded_dy[...], TN).astype(jnp.bfloat16)
    grad_out[STATE:] = through_rows
    for_parity(1, grad_copy, -1, lambda copy: copy.start())

    for tb in range(blocks):
        y, z, d_gated = y_all[span(tb)], z_ref[span(tb)].astype(jnp.float32), kept[span(tb)]
        sig = 1.0 / (1.0 + jnp.exp(-z))
        dz_ref[span(tb)] = (d_gated * y * (sig * (1.0 + z * (1.0 - sig)))).astype(jnp.bfloat16)
        dy = d_gated * (z * sig)
        dx_all[span(tb)] = skip * dy
        product = dy * carried_all[span(tb)]
        total = jnp.zeros(tile, jnp.float32)
        for h in range(heads):
            total = total + jnp.where(
                lane == h, jnp.sum(product[:, lanes(h)], axis=1, keepdims=True), 0.0
            )
        sums[span(tb)] = total
    column_sums[...] = jnp.zeros_like(column_sums)
    db_all[...] = jnp.zeros_like(db_all)
    for tb in range(blocks):
        reached = (tb + 1) * BLOCK
        score = scores[span(tb), 0:reached]
        d_score = None
        row_sums = sums[span(tb)]
        for h in range(heads):
            dy = dy_all[span(tb), lanes(h)]
            decay = decays[h, span(tb), 0:reached]
            d_decayed = decay * dot(dy, x_ref[0:reached, lanes(h)], NT)
            d_score = d_decayed if d_score is None else d_score + d_decayed
            weighed = d_decayed * score
            row_sums = row_sums + jnp.where(
                lane == h, jnp.sum(weighed, axis=1, keepdims=True), 0.0
            )
            column_sums[h : h + 1, 0:reached] += jnp.sum(weighed, axis=0, keepdims=True)
            dx_all[0:reached, lanes(h)] += dot((decay * score).astype(jnp.bfloat16), dy, TN)
        sums[span(tb)] = row_sums
        d_score = d_score.astype(jnp.bfloat16)
        maps_wide[pl.ds(2 * tb * BLOCK + 1, BLOCK, stride=2), :] = dot(
            d_score, b_ref[0:reached], NN
        ) + dot(faded_dy[span(tb)], incoming, NT)
        db_all[0:reached] += dot(d_score, c_ref[span(tb)], TN)

    @pl.when(parity == 1)
    def _():
        for distance in range(1, reach + 1):
            grad_copy(distance).wait_recv()
        total = gathered(grad_far)
        grad_in[...] = total
        grad_relay_out[...] = (
            grad_out[0:STATE].astype(jnp.float32) + through_wide * total
        ).astype(jnp.bfloat16)
        grad_relay().start()

    @pl.when(parity == 0)
    def _():
        grad_relay().wait_recv()
        grad_in[...] = grad_relay_in[...].astype(jnp.float32)

    grad_end = grad_in[...]
    crossing = jnp.sum(grad_end * state_in[...], axis=0, keepdims=True)
    grad_end = grad_end.astype(jnp.bfloat16)
    for tb in range(blocks):
        d_weighted = expanded(0, tb) * dot(b_ref[span(tb)], grad_end, NN)
        dx_ref[span(tb)] = (dx_all[span(tb)] + d_weighted).astype(jnp.bfloat16)
        maps_wide[pl.ds(2 * tb * BLOCK, BLOCK, stride=2), :] = db_all[span(tb)] + dot(
            weighted_x[span(tb)], grad_end, NT
        )
        product = d_weighted * x_ref[span(tb)].astype(jnp.float32)
        total = sums[span(tb)]
        for h in range(heads):
            total = total + jnp.where(
                lane == h + 8, jnp.sum(product[:, lanes(h)], axis=1, keepdims=True), 0.0
            )
        sums[span(tb)] = total
    dmaps_ref[...] = maps_wide[...].astype(jnp.bfloat16)
    turned = sums[...].T
    weight_sums = turned[8:16]
    reach_end = jnp.zeros((8, 1), jnp.float32)
    for h in range(heads):
        reach_end = reach_end + jnp.where(
            iota((8, 1), 0) == h, jnp.sum(crossing[:, lanes(h)], axis=1, keepdims=True), 0.0
        )
    d_last = jnp.sum(weight_sums, axis=1, keepdims=True) + through * reach_end
    d_cumulative = turned[0:8] - column_sums[...] - weight_sums
    d_cumulative = d_cumulative + jnp.where(iota(step.shape, 1) == tokens - 1, d_last, 0.0)
    onward = (iota(square, 0) >= iota(square, 1)).astype(jnp.float32)
    d_exponent = dot(d_cumulative, onward, NN, HIGH)
    d_step = (column_sums[...] + weight_sums) / step - rate * d_exponent
    dstep_ref[...] = (d_step / (1.0 + jnp.exp(-pre)))[0:heads]

    for_parity(0, state_copy, 1, lambda copy: copy.wait_send())
    for_parity(1, grad_copy, -1, lambda copy: copy.wait_send())

    @pl.when(parity == 0)
    def _():
        state_relay().wait_send()

    @pl.when(parity == 1)
    def _():
        grad_relay().wait_send()

    def end_stats(k, _):
        stats_copy(k).wait_send()
        return 0

    lax.fori_loop(1, tensor_count, end_stats, 0)

    def end_ring(step, _):
        for j, way in late_turns:
            late_reduce(way, step, j).wait_send()
            late_gather(way, step, j).wait_send()
        for j, way in early_turns:
            early_reduce(way, step, j).wait_send()
            early_gather(way, step, j).wait_send()
        return 0

    def end_side(step, _):
        for j, way in early_turns:
            halve_copy(way, step, j).wait_send()
            join_copy(way, step, j, own_spots[way]).wait_send()
        return 0

    lax.fori_loop(0, chips - 1, end_ring, 0)
    lax.fori_loop(0, chips, end_side, 0)
    for j, way in late_turns:
        swap_copy(way, j).wait_send()


def deliver_kernel(*refs):
    count = len(refs) // 2
    for source, target in zip(refs[:count], refs[count:]):
        target[...] = source[...].reshape(target.shape)


def deliver(values):
    vmem = pl.BlockSpec(memory_space=pltpu.VMEM)
    return pl.pallas_call(
        deliver_kernel,
        out_shape=tuple(
            jax.ShapeDtypeStruct(v.shape[1:] if v.shape[0] == 1 else v.shape, v.dtype) for v in values
        ),
        in_specs=[vmem] * len(values),
        out_specs=(vmem,) * len(values),
        compiler_params=pltpu.CompilerParams(vmem_limit_bytes=60 << 20),
        name="deliver",
    )(*values)


def on_device(
    ssd_input,
    gate_input,
    state_maps,
    step_raw,
    step_bias,
    decay_rate,
    skip_gain,
    norm_gain,
    out_weight,
    reward_head,
    traj_lengths,
    step_pairs,
):
    tokens, channels = ssd_input.shape
    heads = step_raw.shape[1]
    model_width = out_weight.shape[0]
    seq_count, tensor_count = lax.axis_size("seq"), lax.axis_size("tensor")
    chips = tensor_count // 2
    late_width = model_width // (2 * chips)
    early_width = late_width // 2
    late_pieces, early_pieces = 1, 1
    piece = tokens // (late_pieces + early_pieces)
    steps = chips - 1
    reach = -(-(longest - 1) // tokens)
    bf16, f32 = jnp.bfloat16, jnp.float32

    operands = (
        ssd_input,
        gate_input,
        state_maps.reshape(2 * tokens, STATE),
        step_raw.T,
        step_bias,
        decay_rate,
        skip_gain,
        norm_gain[None, :],
        out_weight,
        reward_head[None, :],
        traj_lengths[None, :],
        step_pairs[None, :],
    )
    vmem = pl.BlockSpec(memory_space=pltpu.VMEM)
    hbm = pl.BlockSpec(memory_space=pltpu.HBM)
    smem = pl.BlockSpec(memory_space=pltpu.SMEM)
    results = pl.pallas_call(
        layer_kernel,
        out_shape=(
            jax.ShapeDtypeStruct((1, tokens), f32),
            jax.ShapeDtypeStruct((tokens, channels), bf16),
            jax.ShapeDtypeStruct((tokens, channels), bf16),
            jax.ShapeDtypeStruct((2 * tokens, STATE), bf16),
            jax.ShapeDtypeStruct((heads, tokens), f32),
        ),
        in_specs=[hbm] * 4 + [smem] * 3 + [hbm] * 5,
        out_specs=(vmem,) * 5,
        scratch_shapes=[
            pltpu.VMEM((model_width, channels), bf16),
            pltpu.VMEM((tokens, channels), bf16),
            pltpu.VMEM((tokens, channels), bf16),
            pltpu.VMEM((2 * tokens, STATE), bf16),
            pltpu.VMEM((heads, tokens), f32),
            pltpu.VMEM((1, channels), f32),
            pltpu.VMEM((1, model_width), f32),
            pltpu.VMEM((1, traj_lengths.shape[0]), jnp.int32),
            pltpu.VMEM((1, step_pairs.shape[0]), jnp.int32),
            pltpu.VMEM((2 * tokens, STATE), f32),
            pltpu.VMEM((tokens, STATE), bf16),
            pltpu.VMEM((tokens, STATE), bf16),
            pltpu.VMEM((tokens, BLOCK), f32),
            pltpu.VMEM((heads, tokens, tokens), f32),
            pltpu.VMEM((tokens, tokens), f32),
            pltpu.VMEM((tokens, channels), f32),
            pltpu.VMEM((tokens, channels), f32),
            pltpu.VMEM((STATE, channels), f32),
            pltpu.VMEM((tokens, channels), bf16),
            pltpu.VMEM((tokens, channels), bf16),
            pltpu.VMEM((tokens, BLOCK), f32),
            pltpu.VMEM((tokens, BLOCK), f32),
            pltpu.VMEM((STATE + 16, channels), bf16),
            pltpu.VMEM((reach, STATE + 16, channels), bf16),
            pltpu.VMEM((STATE + 16, channels), bf16),
            pltpu.VMEM((reach, STATE + 16, channels), bf16),
            pltpu.VMEM((tokens, channels), bf16),
            pltpu.VMEM((tokens, channels), bf16),
            pltpu.VMEM((tokens, channels), f32),
            pltpu.VMEM((tokens, STATE), f32),
            pltpu.VMEM((tokens, BLOCK), f32),
            pltpu.VMEM((8, tokens), f32),
            pltpu.VMEM((tokens, channels), f32),
            pltpu.VMEM((seq_count, 8, tokens), f32),
            pltpu.VMEM((2, steps, late_pieces, piece, late_width), bf16),
            pltpu.VMEM((2, steps, late_pieces, piece, late_width), bf16),
            pltpu.VMEM((2, late_pieces, piece, late_width), bf16),
            pltpu.VMEM((2, late_pieces, piece, late_width), bf16),
            pltpu.VMEM((chips, 2, late_pieces, piece, late_width), bf16),
            pltpu.VMEM((2, steps, early_pieces, piece, early_width), bf16),
            pltpu.VMEM((2, steps, early_pieces, piece, early_width), bf16),
            pltpu.VMEM((2, chips, early_pieces, piece, early_width), bf16),
            pltpu.VMEM((2, chips, early_pieces, piece, early_width), bf16),
            pltpu.VMEM((chips, 2, 2, early_pieces, piece, early_width), bf16),
            pltpu.VMEM((8, tokens), f32),
            pltpu.VMEM((tensor_count, 8, tokens), f32),
            pltpu.VMEM((8, tokens), f32),
            pltpu.VMEM((STATE, channels), bf16),
            pltpu.VMEM((STATE, channels), bf16),
            pltpu.VMEM((STATE, channels), bf16),
            pltpu.VMEM((STATE, channels), bf16),
            pltpu.VMEM((STATE, channels), f32),
            pltpu.VMEM((tokens, channels), f32),
            pltpu.VMEM((tokens, BLOCK), f32),
            pltpu.VMEM((tokens, BLOCK), f32),
            pltpu.SemaphoreType.DMA((9,)),
            pltpu.SemaphoreType.DMA((2,)),
            pltpu.SemaphoreType.DMA((2,)),
            pltpu.SemaphoreType.DMA((reach,)),
            pltpu.SemaphoreType.DMA((reach,)),
            pltpu.SemaphoreType.DMA((reach,)),
            pltpu.SemaphoreType.DMA((reach,)),
            pltpu.SemaphoreType.DMA((2, steps, late_pieces)),
            pltpu.SemaphoreType.DMA((2, steps, late_pieces)),
            pltpu.SemaphoreType.DMA((2, late_pieces)),
            pltpu.SemaphoreType.DMA((2, late_pieces)),
            pltpu.SemaphoreType.DMA((2, steps, late_pieces)),
            pltpu.SemaphoreType.DMA((2, steps, late_pieces)),
            pltpu.SemaphoreType.DMA((2, steps, early_pieces)),
            pltpu.SemaphoreType.DMA((2, steps, early_pieces)),
            pltpu.SemaphoreType.DMA((2, steps, early_pieces)),
            pltpu.SemaphoreType.DMA((2, steps, early_pieces)),
            pltpu.SemaphoreType.DMA((2, chips, early_pieces)),
            pltpu.SemaphoreType.DMA((2, chips, early_pieces)),
            pltpu.SemaphoreType.DMA((2, chips, early_pieces)),
            pltpu.SemaphoreType.DMA((2, chips, early_pieces)),
            pltpu.SemaphoreType.DMA((tensor_count,)),
            pltpu.SemaphoreType.DMA((tensor_count,)),
            pltpu.SemaphoreType.DMA((seq_count,)),
            pltpu.SemaphoreType.DMA((seq_count,)),
        ],
        compiler_params=pltpu.CompilerParams(
            collective_id=0, has_side_effects=True, vmem_limit_bytes=60 << 20
        ),
        name="layer",
    )(*operands)
    rewards, dx, dz, dmaps, dstep = deliver(results)
    return (
        rewards,
        dx,
        dz,
        dmaps.reshape(tokens, 2, STATE),
        dstep.T,
    )


def solution(mesh):
    return jax.shard_map(
        on_device,
        mesh=mesh,
        in_specs=(
            P("seq", "tensor"),
            P("seq", "tensor"),
            P("seq", None, "tensor"),
            P("seq", "tensor"),
            P("tensor"),
            P("tensor"),
            P("tensor"),
            P("tensor"),
            P(None, "tensor"),
            P(),
            P(),
            P(),
        ),
        out_specs=(
            P("seq"),
            P("seq", "tensor"),
            P("seq", "tensor"),
            P("seq", None, "tensor"),
            P("seq", "tensor"),
        ),
        check_vma=False,
    )
```

```python
import jax
import jax.numpy as jnp
from jax import lax
from jax.experimental import pallas as pl
from jax.experimental.pallas import tpu as pltpu
from jax.sharding import PartitionSpec as P

STATE = 128
BLOCK = 128

norm_eps = 1e-05
loss_scale = 64.0
longest = 1152
MESH = pl.DeviceIdType.MESH
HIGH = lax.Precision.HIGHEST
NT = ((1,), (1,))
NN = ((1,), (0,))
TN = ((0,), (0,))


def dot(left, right, dims, precision=None):
    return lax.dot_general(
        left, right, (dims, ((), ())), preferred_element_type=jnp.float32, precision=precision
    )


def iota(shape, axis):
    return lax.broadcasted_iota(jnp.int32, shape, axis)


def three_terms(value):
    high = value.astype(jnp.bfloat16).astype(jnp.float32)
    rest = value - high
    middle = rest.astype(jnp.bfloat16).astype(jnp.float32)
    return jnp.concatenate([high, middle, rest - middle], axis=0).astype(jnp.bfloat16)


def exact_dot(value, right, dims):
    result = dot(three_terms(value), right, dims)
    return result[0:8] + result[8:16] + result[16:24]


def layer_kernel(
    x_hbm,
    z_hbm,
    maps_hbm,
    raw_hbm,
    bias_ref,
    rate_ref,
    skip_ref,
    gain_hbm,
    weight_hbm,
    head_hbm,
    length_hbm,
    pairs_hbm,
    reward_out,
    dx_ref,
    dz_ref,
    dmaps_ref,
    dstep_ref,
    weight,
    x_ref,
    z_ref,
    maps_ref,
    raw_ref,
    gain_ref,
    head_ref,
    length_ref,
    pairs_ref,
    maps_wide,
    b_ref,
    c_ref,
    columns,
    decays,
    scores,
    y_all,
    carried_all,
    state_in,
    mixed,
    weighted_x,
    mate_all,
    sign_all,
    state_out,
    state_far,
    grad_out,
    grad_far,
    dy_all,
    faded_dy,
    dx_all,
    db_all,
    sums,
    column_sums,
    back,
    rewards,
    late_out,
    late_moving,
    swap_out,
    swap_in,
    late_hidden,
    early_out,
    early_moving,
    halve_out,
    halve_in,
    early_hidden,
    own_stats,
    far_stats,
    own_reward,
    state_relay_out,
    state_relay_in,
    grad_relay_out,
    grad_relay_in,
    grad_in,
    kept,
    facts,
    factors,
    load_sems,
    relay_send,
    relay_recv,
    state_send,
    state_recv,
    grad_send,
    grad_recv,
    late_reduce_send,
    late_reduce_recv,
    swap_send,
    swap_recv,
    late_gather_send,
    late_gather_recv,
    early_reduce_send,
    early_reduce_recv,
    early_gather_send,
    early_gather_recv,
    halve_send,
    halve_recv,
    join_send,
    join_recv,
    stats_send,
    stats_recv,
    reward_send,
    reward_recv,
):
    seq, tensor = lax.axis_index("seq"), lax.axis_index("tensor")
    seq_count, tensor_count = lax.axis_size("seq"), lax.axis_size("tensor")
    chips = tensor_count // 2
    place, side = lax.rem(tensor, chips), tensor // chips
    base = side * chips
    up = (seq, base + lax.rem(place + 1, chips))
    down = (seq, base + lax.rem(place + chips - 1, chips))
    across = (seq, (1 - side) * chips + place)
    ways = (up, down)
    tokens, channels = x_ref.shape
    model_width = weight.shape[0]
    late_pieces, piece, late_width = late_hidden.shape[2:]
    early_pieces, _, early_width = early_hidden.shape[3:]
    cut = late_pieces * piece
    width = channels // (raw_ref.shape[0])
    heads = channels // width
    blocks = tokens // BLOCK
    reach = state_far.shape[0]
    pair_tiles = pairs_ref.shape[1] // BLOCK

    loads = [
        pltpu.make_async_copy(source, target, load_sems.at[k])
        for k, (source, target) in enumerate(
            [
                (raw_hbm, raw_ref),
                (length_hbm, length_ref),
                (maps_hbm, maps_ref),
                (x_hbm, x_ref),
                (pairs_hbm, pairs_ref),
                (head_hbm, head_ref),
                (gain_hbm, gain_ref),
                (z_hbm, z_ref),
                (weight_hbm, weight),
            ]
        )
    ]
    for load in loads:
        load.start()
    barrier = pltpu.get_barrier_semaphore()

    def greet_tensor(k, _):
        other = lax.rem(tensor + k, tensor_count)
        pl.semaphore_signal(barrier, inc=1, device_id=(seq, other), device_id_type=MESH)
        return 0

    def greet_seq(k, _):
        other = lax.rem(seq + k, seq_count)
        pl.semaphore_signal(barrier, inc=1, device_id=(other, tensor), device_id_type=MESH)
        return 0

    lax.fori_loop(1, tensor_count, greet_tensor, 0)
    lax.fori_loop(1, seq_count, greet_seq, 0)

    def span(tb):
        return slice(tb * BLOCK, (tb + 1) * BLOCK)

    def lanes(h):
        return slice(h * width, (h + 1) * width)

    def per_head(ref):
        row = lax.rem(iota((8, 1), 0), heads)
        return sum(jnp.where(row == h, ref[h], 0.0) for h in range(heads))

    bias, rate = per_head(bias_ref), per_head(rate_ref)
    for load in loads[:2]:
        load.wait()
    pre = jnp.concatenate([raw_ref[...], raw_ref[...]], axis=0) + bias
    step = jnp.maximum(pre, 0.0) + jnp.log1p(jnp.exp(-jnp.abs(pre)))
    exponent = -step * rate
    square = (tokens, tokens)
    upto = jnp.where(iota(square, 0) <= iota(square, 1), 1.0, 0.0).astype(jnp.bfloat16)
    cumulative = exact_dot(exponent, upto, NN)
    count = length_ref.shape[1]
    openings = jnp.sum(
        jnp.where(
            iota((count, count), 1) < iota((count, count), 0),
            length_ref[...].astype(jnp.float32),
            0.0,
        ),
        axis=1,
        keepdims=True,
    )
    position = (iota((count, tokens), 1) + seq * tokens).astype(jnp.float32)
    block_start = (iota((count, tokens), 0) * 0 + seq * tokens).astype(jnp.float32)
    segment = jnp.sum(
        jnp.where((openings <= position) & (openings >= block_start), 1.0, 0.0),
        axis=0,
        keepdims=True,
    )
    last_segment = segment[:, tokens - 1 :]
    last_cumulative = cumulative[:, tokens - 1 :]
    end_weight = jnp.where(
        jnp.broadcast_to(segment == last_segment, step.shape),
        jnp.exp(last_cumulative - cumulative),
        0.0,
    )
    end_weight = end_weight * step
    first_weight = jnp.where(
        jnp.broadcast_to(segment == 0.0, step.shape), jnp.exp(cumulative), 0.0
    )
    through = jnp.where(last_segment == 0.0, jnp.exp(last_cumulative), 0.0)
    segment_rows = jnp.broadcast_to(segment, step.shape)
    columns[...] = jnp.concatenate(
        [
            end_weight,
            first_weight,
            cumulative,
            segment_rows,
            jnp.zeros((BLOCK - 32, tokens), jnp.float32),
        ],
        axis=0,
    ).T

    def column(kind, h, tb):
        return columns[span(tb), kind * 8 + h : kind * 8 + h + 1]

    def expanded(kind, tb):
        return jnp.concatenate(
            [jnp.broadcast_to(column(kind, h, tb), (BLOCK, width)) for h in range(heads)], axis=1
        )

    through_wide = jnp.concatenate(
        [jnp.broadcast_to(through[h : h + 1], (1, width)) for h in range(heads)], axis=1
    )
    through_high = through_wide.astype(jnp.bfloat16).astype(jnp.float32)
    tail_shape = (16, channels)
    through_rows = jnp.where(
        iota(tail_shape, 0) == 0,
        through_high,
        jnp.where(iota(tail_shape, 0) == 1, through_wide - through_high, 0.0),
    ).astype(jnp.bfloat16)

    def far_copy(source, target, send, recv, distance, direction):
        return pltpu.make_async_remote_copy(
            src_ref=source,
            dst_ref=target.at[distance - 1],
            send_sem=send.at[distance - 1],
            recv_sem=recv.at[distance - 1],
            device_id=(lax.rem(seq + seq_count + direction * distance, seq_count), tensor),
            device_id_type=MESH,
        )

    def state_copy(distance):
        return far_copy(state_out, state_far, state_send, state_recv, distance, 1)

    def grad_copy(distance):
        return far_copy(grad_out, grad_far, grad_send, grad_recv, distance, -1)

    def relay_copy(buffer_out, buffer_in, send, recv, direction):
        return pltpu.make_async_remote_copy(
            src_ref=buffer_out,
            dst_ref=buffer_in,
            send_sem=send,
            recv_sem=recv,
            device_id=(lax.rem(seq + seq_count + direction, seq_count), tensor),
            device_id_type=MESH,
        )

    def state_relay():
        return relay_copy(state_relay_out, state_relay_in, relay_send.at[0], relay_recv.at[0], 1)

    def grad_relay():
        return relay_copy(grad_relay_out, grad_relay_in, relay_send.at[1], relay_recv.at[1], -1)

    parity = lax.rem(seq, 2)

    def for_parity(taker, copy, direction, act):
        for kind in range(2):

            @pl.when(parity == kind)
            def _():
                for distance in range(1, reach + 1):
                    if (kind + direction * distance) % 2 == taker:
                        act(copy(distance))

    def gathered(far):
        total, carry = None, None
        for k in range(reach):
            value = far[k, 0:STATE].astype(jnp.float32)
            passed = far[k, STATE : STATE + 1].astype(jnp.float32) + far[
                k, STATE + 1 : STATE + 2
            ].astype(jnp.float32)
            if total is None:
                total, carry = value, passed
            else:
                total = total + carry * value
                carry = carry * passed
        return total

    loads[2].wait()
    maps_wide[...] = maps_ref[...].astype(jnp.float32)
    b_ref[...] = maps_wide[pl.ds(0, tokens, stride=2), :].astype(jnp.bfloat16)
    c_ref[...] = maps_wide[pl.ds(1, tokens, stride=2), :].astype(jnp.bfloat16)
    loads[3].wait()
    for tb in range(blocks):
        weighted_x[span(tb)] = (
            x_ref[span(tb)].astype(jnp.float32) * expanded(0, tb)
        ).astype(jnp.bfloat16)
    state_out[0:STATE] = dot(b_ref[...], weighted_x[...], TN).astype(jnp.bfloat16)
    state_out[STATE:] = through_rows
    pl.semaphore_wait(barrier, tensor_count + seq_count - 2)
    for_parity(0, state_copy, 1, lambda copy: copy.start())

    for tb in range(blocks):
        reached = (tb + 1) * BLOCK
        score = dot(c_ref[span(tb)], b_ref[0:reached], NT)
        scores[span(tb), 0:reached] = score
        shape = (BLOCK, reached)
        allowed = (column(3, 0, tb) == segment[:, 0:reached]) & (
            iota(shape, 1) <= iota(shape, 0) + tb * BLOCK
        )
        for h in range(heads):
            spread = column(2, h, tb) - cumulative[h : h + 1, 0:reached]
            decay = jnp.exp(jnp.where(allowed, spread, -1e30)) * step[h : h + 1, 0:reached]
            decays[h, span(tb), 0:reached] = decay
            y_all[span(tb), lanes(h)] = dot(
                (decay * score).astype(jnp.bfloat16), x_ref[0:reached, lanes(h)], NN
            )

    for load in loads[4:8]:
        load.wait()
    reward_row = head_ref[...]
    high = reward_row.astype(jnp.bfloat16).astype(jnp.float32)
    rest = reward_row - high
    middle = rest.astype(jnp.bfloat16).astype(jnp.float32)
    term = iota((8, model_width), 0)
    terms = jnp.where(
        term == 0,
        high,
        jnp.where(term == 1, middle, jnp.where(term == 2, rest - middle, 0.0)),
    ).astype(jnp.bfloat16)
    loads[8].wait()
    reward_channels = jnp.sum(dot(terms, weight[...], NN), axis=0, keepdims=True)

    @pl.when(parity == 0)
    def _():
        for distance in range(1, reach + 1):
            state_copy(distance).wait_recv()
        total = gathered(state_far)
        state_in[...] = total
        state_relay_out[...] = (
            state_out[0:STATE].astype(jnp.float32) + through_wide * total
        ).astype(jnp.bfloat16)
        state_relay().start()

    @pl.when(parity == 1)
    def _():
        state_relay().wait_recv()
        state_in[...] = state_relay_in[...].astype(jnp.float32)

    incoming = state_in[...].astype(jnp.bfloat16)
    gain = gain_ref[...]
    skip = jnp.concatenate([jnp.full((1, width), skip_ref[h]) for h in range(heads)], axis=1)

    def gating(tb):
        y = y_all[span(tb)]
        z = z_ref[span(tb)].astype(jnp.float32)
        sig = 1.0 / (1.0 + jnp.exp(-z))
        silu = z * sig
        gated = y * silu
        mean_square = jnp.sum(gated * gated, axis=1, keepdims=True) / channels
        return y, z, sig, silu, gated, lax.rsqrt(mean_square + norm_eps)

    for tb in range(blocks):
        carried = expanded(1, tb) * dot(c_ref[span(tb)], incoming, NN)
        carried_all[span(tb)] = carried
        y_all[span(tb)] = (
            y_all[span(tb)] + carried + skip * x_ref[span(tb)].astype(jnp.float32)
        )
        _, _, _, _, gated, inverse = gating(tb)
        mixed[span(tb)] = (gated * inverse * gain).astype(jnp.bfloat16)

    tile = (BLOCK, BLOCK)
    unroll = 4
    def search(tb):
        token = iota(tile, 0) + (seq * tokens + tb * BLOCK)

        def find(i, total):
            for k in range(unroll):
                start = pl.multiple_of((i * unroll + k) * BLOCK, BLOCK)
                row = pairs_ref[0:1, pl.ds(start, BLOCK)]
                order = (iota(tile, 1) + start).astype(jnp.float32)
                total = total + jnp.where(row == token, order, 0.0)
            return total

        zero = jnp.zeros(tile, jnp.float32)
        order = jnp.sum(
            lax.fori_loop(0, pair_tiles // unroll, find, zero), axis=1, keepdims=True
        )
        odd = order - 2.0 * jnp.floor(order * 0.5)
        other = jnp.broadcast_to(order + 1.0 - 2.0 * odd, tile)

        def fetch(i, total):
            for k in range(unroll):
                start = pl.multiple_of((i * unroll + k) * BLOCK, BLOCK)
                row = pairs_ref[0:1, pl.ds(start, BLOCK)].astype(jnp.float32)
                order = (iota(tile, 1) + start).astype(jnp.float32)
                total = total + jnp.where(other == order, row, 0.0)
            return total

        mate = jnp.sum(
            lax.fori_loop(0, pair_tiles // unroll, fetch, zero), axis=1, keepdims=True
        )
        mate_all[span(tb)] = jnp.broadcast_to(mate, tile)
        sign_all[span(tb)] = jnp.broadcast_to(2.0 * odd - 1.0, tile)

    last = chips - 2

    def chunk(way, distance):
        return lax.rem(place + chips + (distance if way == 0 else -distance), chips)

    def part_half(way, i):
        odd = lax.rem(i, 2)
        return odd if way == 0 else 1 - odd

    def reduce_spot(way, i):
        return chunk(way, chips // 2 - lax.div(i + 1, 2)), part_half(way, i)

    def gather_spot(way, i):
        return chunk(way, -lax.div(i, 2)), part_half(way, i)

    def late_rows(spot):
        index, part = spot
        return pl.ds(pl.multiple_of((index * 2 + part) * late_width, late_width), late_width)

    def early_rows(spot, owner):
        index, part = spot
        start = ((index * 2 + owner) * 2 + part) * early_width
        return pl.ds(pl.multiple_of(start, early_width), early_width)

    def late_part(spot):
        return dot(mixed[0:cut], weight[late_rows(spot), :], NT)

    def early_part(spot, owner):
        return dot(mixed[cut:], weight[early_rows(spot, owner), :], NT)

    def remote(source, target, send, recv, device):
        return pltpu.make_async_remote_copy(
            src_ref=source,
            dst_ref=target,
            send_sem=send,
            recv_sem=recv,
            device_id=device,
            device_id_type=MESH,
        )

    def late_reduce(way, i, j):
        return remote(
            late_out.at[way, i, j],
            late_moving.at[way, i, j],
            late_reduce_send.at[way, i, j],
            late_reduce_recv.at[way, i, j],
            ways[way],
        )

    def early_reduce(way, i, j):
        return remote(
            early_out.at[way, i, j],
            early_moving.at[way, i, j],
            early_reduce_send.at[way, i, j],
            early_reduce_recv.at[way, i, j],
            ways[way],
        )

    def halve_copy(way, i, j):
        return remote(
            halve_out.at[way, i, j],
            halve_in.at[way, i, j],
            halve_send.at[way, i, j],
            halve_recv.at[way, i, j],
            across,
        )

    def swap_copy(way, j):
        return remote(
            swap_out.at[way, j], swap_in.at[way, j], swap_send.at[way, j], swap_recv.at[way, j], across
        )

    def late_gather(way, i, j):
        index, part = gather_spot(way, i)
        spot = late_hidden.at[index, part, j]
        return remote(
            spot, spot, late_gather_send.at[way, i, j], late_gather_recv.at[way, i, j], ways[way]
        )

    def early_gather(way, i, j):
        index, part = gather_spot(way, i)
        spot = early_hidden.at[index, side, part, j]
        return remote(
            spot, spot, early_gather_send.at[way, i, j], early_gather_recv.at[way, i, j], ways[way]
        )

    def arrived_spot(way, i):
        return chunk(way, -lax.div(i, 2) - 1), part_half(way, i)

    def join_copy(way, i, j, at):
        index, part = at
        spot = early_hidden.at[index, side, part, j]
        return remote(spot, spot, join_send.at[way, i, j], join_recv.at[way, i, j], across)

    late_turns = [(j, way) for j in range(late_pieces) for way in range(2)]
    early_turns = [(j, way) for j in range(early_pieces) for way in range(2)]

    def cut_piece(value, j):
        rows = value.shape[0] // (late_pieces if value.shape[1] == late_width else early_pieces)
        return value[j * rows : (j + 1) * rows]

    def start_halving(i, at=None):
        for way in range(2):
            part = early_part(reduce_spot(way, i) if at is None else at[way], 1 - side)
            for j in range(early_pieces):
                halve_out[way, i, j] = cut_piece(part, j).astype(jnp.bfloat16)
                halve_copy(way, i, j).start()

    def start_late(i):
        for way in range(2):
            part = late_part(reduce_spot(way, i))
            for j in range(late_pieces):
                late_out[way, i, j] = cut_piece(part, j).astype(jnp.bfloat16)
                late_reduce(way, i, j).start()

    def start_early(i):
        parts = [early_part(reduce_spot(way, i), side) for way in range(2)]
        for j, way in early_turns:
            halve_copy(way, i, j).wait_recv()
            early_out[way, i, j] = (
                cut_piece(parts[way], j) + halve_in[way, i, j].astype(jnp.float32)
            ).astype(jnp.bfloat16)
            early_reduce(way, i, j).start()

    start_halving(0)
    start_late(0)
    start_halving(1)
    start_late(1)
    start_halving(2)
    start_early(0)
    start_halving(3)
    start_early(1)

    along = exact_dot(jnp.broadcast_to(reward_channels, (8, channels)), mixed[...], NT)

    own_spots = [(place, way) for way in range(2)]

    def reduce_work(i):
        late_parts = [late_part(reduce_spot(way, i + 2)) for way in range(2)]
        early_parts = [early_part(reduce_spot(way, i + 2), side) for way in range(2)]

        def late_turn(j, way):
            late_reduce(way, i, j).wait_recv()
            late_out[way, i + 2, j] = (
                late_moving[way, i, j].astype(jnp.float32) + cut_piece(late_parts[way], j)
            ).astype(jnp.bfloat16)
            late_reduce(way, i + 2, j).start()

        def early_turn(j, way):
            halve_copy(way, i + 2, j).wait_recv()
            early_reduce(way, i, j).wait_recv()
            early_out[way, i + 2, j] = (
                early_moving[way, i, j].astype(jnp.float32)
                + cut_piece(early_parts[way], j)
                + halve_in[way, i + 2, j].astype(jnp.float32)
            ).astype(jnp.bfloat16)
            early_reduce(way, i + 2, j).start()

        for k in range(max(len(late_turns), len(early_turns))):
            if k < len(late_turns):
                late_turn(*late_turns[k])
            if k < len(early_turns):
                early_turn(*early_turns[k])

    def reduce_step(i, _):
        start_halving(i + 4)
        reduce_work(i)
        return 0

    for tb in range(blocks):
        reduce_step(tb, 0)
        search(tb)
    start_halving(last + 1, own_spots)
    lax.fori_loop(last - 3, last - 1, lambda i, _: reduce_work(i) or 0, 0)

    late_parts = [late_part(own_spots[way]) for way in range(2)]
    early_parts = [early_part(own_spots[way], side) for way in range(2)]
    for j, way in late_turns:
        late_reduce(1 - way, last - 1, j).wait_recv()
        late_reduce(way, last, j).wait_recv()
        swap_out[way, j] = (
            late_moving[way, last, j].astype(jnp.float32)
            + late_moving[1 - way, last - 1, j].astype(jnp.float32)
            + cut_piece(late_parts[way], j)
        ).astype(jnp.bfloat16)
        swap_copy(way, j).start()
    for j, way in early_turns:
        halve_copy(way, last + 1, j).wait_recv()
        early_reduce(1 - way, last - 1, j).wait_recv()
        early_reduce(way, last, j).wait_recv()
        early_hidden[place, side, way, j] = (
            early_moving[way, last, j].astype(jnp.float32)
            + early_moving[1 - way, last - 1, j].astype(jnp.float32)
            + cut_piece(early_parts[way], j)
            + halve_in[way, last + 1, j].astype(jnp.float32)
        ).astype(jnp.bfloat16)
        early_gather(way, 0, j).start()
        early_gather(1 - way, 1, j).start()
    for j, way in late_turns:
        swap_copy(way, j).wait_recv()
        late_hidden[place, way, j] = (
            swap_out[way, j].astype(jnp.float32) + swap_in[way, j].astype(jnp.float32)
        ).astype(jnp.bfloat16)
        late_gather(way, 0, j).start()
        late_gather(1 - way, 1, j).start()
    for j, way in early_turns:
        join_copy(way, 0, j, own_spots[way]).start()

    def squares(read, columns_count):
        total = None
        for way in range(2):
            value = read(way).astype(jnp.float32)
            total = value * value if total is None else total + value * value
        return dot(jnp.ones((8, columns_count), jnp.float32), total, NT, HIGH)

    late_squares = squares(lambda way: late_hidden[place, way].reshape(cut, late_width), late_width)
    early_squares = squares(
        lambda way: early_hidden[place, side, way].reshape(tokens - cut, early_width), early_width
    )
    is_along = iota((8, tokens), 0) == 0
    own_stats[...] = jnp.where(
        is_along, along, jnp.concatenate([0.5 * late_squares, early_squares], axis=1)
    )

    def stats_copy(k):
        return remote(
            own_stats,
            far_stats.at[k],
            stats_send.at[k],
            stats_recv.at[k],
            (seq, lax.rem(tensor + k, tensor_count)),
        )

    def reward_copy(k):
        return remote(
            own_reward,
            rewards.at[seq],
            reward_send.at[k],
            reward_recv.at[k],
            (lax.rem(seq + k, seq_count), tensor),
        )

    def start_stats(k, _):
        stats_copy(k).start()
        return 0

    lax.fori_loop(1, tensor_count, start_stats, 0)

    def late_back(spot):
        index, part = spot
        return dot(late_hidden[index, part].reshape(cut, late_width), weight[late_rows(spot), :], NN)

    def early_back(spot, owner):
        index, part = spot
        return dot(
            early_hidden[index, owner, part].reshape(tokens - cut, early_width),
            weight[early_rows(spot, owner), :],
            NN,
        )

    def add_joined(i, spots):
        for j, way in early_turns:
            join_copy(way, i, j, spots[way]).wait_recv()
        back[cut:] += early_back(spots[0], 1 - side) + early_back(spots[1], 1 - side)

    back[0:cut] = late_back(own_spots[0]) + late_back(own_spots[1])
    back[cut:] = early_back(own_spots[0], side) + early_back(own_spots[1], side)

    def take(i, forward):
        spots = [arrived_spot(way, i) for way in range(2)]
        for k in range(max(len(late_turns), len(early_turns))):
            if k < len(early_turns):
                j, way = early_turns[k]
                early_gather(way, i, j).wait_recv()
                if forward:
                    early_gather(way, i + 2, j).start()
                join_copy(way, i + 1, j, spots[way]).start()
            if k < len(late_turns):
                j, way = late_turns[k]
                late_gather(way, i, j).wait_recv()
                if forward:
                    late_gather(way, i + 2, j).start()
        back[0:cut] += late_back(spots[0]) + late_back(spots[1])
        back[cut:] += early_back(spots[0], side) + early_back(spots[1], side)

    def gather_step(i, _):
        take(i, True)
        add_joined(i, [arrived_spot(way, i - 1) for way in range(2)])
        return 0

    take(0, True)
    add_joined(0, own_spots)
    gather_step(1, 0)

    def add_stats(k, total):
        stats_copy(k).wait_recv()
        return total + far_stats[k]

    stats = lax.fori_loop(1, tensor_count, add_stats, own_stats[...])
    scale = jnp.sqrt(stats[1:2] / model_width + norm_eps)
    own_reward[...] = jnp.broadcast_to(stats[0:1] / scale, own_reward.shape)
    rewards[seq] = own_reward[...]

    facts[...] = jnp.concatenate(
        [stats, jnp.broadcast_to(scale, stats.shape), own_reward[...]]
        + [jnp.zeros((BLOCK - 24, tokens), jnp.float32)],
        axis=0,
    ).T
    lane = iota(tile, 1)

    def match(tb):
        mate = mate_all[span(tb)].astype(jnp.int32)
        sign = sign_all[span(tb), 0:1]

        def look(i, total):
            for k in range(blocks):
                row = rewards[i, 0:1, k * BLOCK : (k + 1) * BLOCK]
                total = total + jnp.where(mate == lane + (i * tokens + k * BLOCK), row, 0.0)
            return total

        mate_reward = jnp.sum(
            lax.fori_loop(0, seq_count, look, jnp.zeros(tile, jnp.float32)), axis=1, keepdims=True
        )
        own_along = facts[span(tb), 0:1]
        own_scale = facts[span(tb), 8:9]
        push = sign * (facts[span(tb), 16:17] - mate_reward)
        pair_grad = sign * (loss_scale / (1.0 + jnp.exp(-push)))
        hidden_factor = own_along / (model_width * own_scale * own_scale)
        factors[span(tb)] = jnp.where(lane == 0, pair_grad / own_scale, hidden_factor)

    def start_reward(k, _):
        reward_copy(k).start()
        return 0

    lax.fori_loop(1, seq_count, start_reward, 0)
    lax.fori_loop(2, last - 2, gather_step, 0)

    def end_reward(k, _):
        reward_copy(k).wait()
        return 0

    lax.fori_loop(1, seq_count, end_reward, 0)
    match(0)
    gather_step(last - 2, 0)
    for i in (last - 1, last):
        match(i - last + 2)
        take(i, False)
        add_joined(i, [arrived_spot(way, i - 1) for way in range(2)])
    add_joined(last + 1, [arrived_spot(way, last) for way in range(2)])


    reward_out[...] = own_reward[0:1]

    for tb in range(blocks):
        own_factor, hidden_factor = factors[span(tb), 0:1], factors[span(tb), 1:2]
        y, z, sig, silu, gated, inverse = gating(tb)
        d_gained = gain * (
            own_factor * (reward_channels - hidden_factor * back[span(tb)])
        )
        shared = jnp.sum(gated * d_gained, axis=1, keepdims=True) / channels
        d_gated = inverse * d_gained - gated * (inverse * inverse * inverse * shared)
        kept[span(tb)] = d_gated
        dy = d_gated * silu
        dy_all[span(tb)] = dy.astype(jnp.bfloat16)
        faded_dy[span(tb)] = (dy * expanded(1, tb)).astype(jnp.bfloat16)
    grad_out[0:STATE] = dot(c_ref[...], faded_dy[...], TN).astype(jnp.bfloat16)
    grad_out[STATE:] = through_rows
    for_parity(1, grad_copy, -1, lambda copy: copy.start())

    for tb in range(blocks):
        y, z, d_gated = y_all[span(tb)], z_ref[span(tb)].astype(jnp.float32), kept[span(tb)]
        sig = 1.0 / (1.0 + jnp.exp(-z))
        dz_ref[span(tb)] = (d_gated * y * (sig * (1.0 + z * (1.0 - sig)))).astype(jnp.bfloat16)
        dy = d_gated * (z * sig)
        dx_all[span(tb)] = skip * dy
        product = dy * carried_all[span(tb)]
        total = jnp.zeros(tile, jnp.float32)
        for h in range(heads):
            total = total + jnp.where(
                lane == h, jnp.sum(product[:, lanes(h)], axis=1, keepdims=True), 0.0
            )
        sums[span(tb)] = total
    column_sums[...] = jnp.zeros_like(column_sums)
    db_all[...] = jnp.zeros_like(db_all)
    for tb in range(blocks):
        reached = (tb + 1) * BLOCK
        score = scores[span(tb), 0:reached]
        d_score = None
        row_sums = sums[span(tb)]
        for h in range(heads):
            dy = dy_all[span(tb), lanes(h)]
            decay = decays[h, span(tb), 0:reached]
            d_decayed = decay * dot(dy, x_ref[0:reached, lanes(h)], NT)
            d_score = d_decayed if d_score is None else d_score + d_decayed
            weighed = d_decayed * score
            row_sums = row_sums + jnp.where(
                lane == h, jnp.sum(weighed, axis=1, keepdims=True), 0.0
            )
            column_sums[h : h + 1, 0:reached] += jnp.sum(weighed, axis=0, keepdims=True)
            dx_all[0:reached, lanes(h)] += dot((decay * score).astype(jnp.bfloat16), dy, TN)
        sums[span(tb)] = row_sums
        d_score = d_score.astype(jnp.bfloat16)
        maps_wide[pl.ds(2 * tb * BLOCK + 1, BLOCK, stride=2), :] = dot(
            d_score, b_ref[0:reached], NN
        ) + dot(faded_dy[span(tb)], incoming, NT)
        db_all[0:reached] += dot(d_score, c_ref[span(tb)], TN)

    @pl.when(parity == 1)
    def _():
        for distance in range(1, reach + 1):
            grad_copy(distance).wait_recv()
        total = gathered(grad_far)
        grad_in[...] = total
        grad_relay_out[...] = (
            grad_out[0:STATE].astype(jnp.float32) + through_wide * total
        ).astype(jnp.bfloat16)
        grad_relay().start()

    @pl.when(parity == 0)
    def _():
        grad_relay().wait_recv()
        grad_in[...] = grad_relay_in[...].astype(jnp.float32)

    grad_end = grad_in[...]
    crossing = jnp.sum(grad_end * state_in[...], axis=0, keepdims=True)
    grad_end = grad_end.astype(jnp.bfloat16)
    for tb in range(blocks):
        d_weighted = expanded(0, tb) * dot(b_ref[span(tb)], grad_end, NN)
        dx_ref[span(tb)] = (dx_all[span(tb)] + d_weighted).astype(jnp.bfloat16)
        maps_wide[pl.ds(2 * tb * BLOCK, BLOCK, stride=2), :] = db_all[span(tb)] + dot(
            weighted_x[span(tb)], grad_end, NT
        )
        product = d_weighted * x_ref[span(tb)].astype(jnp.float32)
        total = sums[span(tb)]
        for h in range(heads):
            total = total + jnp.where(
                lane == h + 8, jnp.sum(product[:, lanes(h)], axis=1, keepdims=True), 0.0
            )
        sums[span(tb)] = total
    dmaps_ref[...] = maps_wide[...].astype(jnp.bfloat16)
    turned = sums[...].T
    weight_sums = turned[8:16]
    reach_end = jnp.zeros((8, 1), jnp.float32)
    for h in range(heads):
        reach_end = reach_end + jnp.where(
            iota((8, 1), 0) == h, jnp.sum(crossing[:, lanes(h)], axis=1, keepdims=True), 0.0
        )
    d_last = jnp.sum(weight_sums, axis=1, keepdims=True) + through * reach_end
    d_cumulative = turned[0:8] - column_sums[...] - weight_sums
    d_cumulative = d_cumulative + jnp.where(iota(step.shape, 1) == tokens - 1, d_last, 0.0)
    onward = jnp.where(iota(square, 0) >= iota(square, 1), 1.0, 0.0).astype(jnp.bfloat16)
    d_exponent = exact_dot(d_cumulative, onward, NN)
    d_step = (column_sums[...] + weight_sums) / step - rate * d_exponent
    dstep_ref[...] = (d_step / (1.0 + jnp.exp(-pre)))[0:heads]

    for_parity(0, state_copy, 1, lambda copy: copy.wait_send())
    for_parity(1, grad_copy, -1, lambda copy: copy.wait_send())

    @pl.when(parity == 0)
    def _():
        state_relay().wait_send()

    @pl.when(parity == 1)
    def _():
        grad_relay().wait_send()

    def end_stats(k, _):
        stats_copy(k).wait_send()
        return 0

    lax.fori_loop(1, tensor_count, end_stats, 0)

    def end_ring(step, _):
        for j, way in late_turns:
            late_reduce(way, step, j).wait_send()
            late_gather(way, step, j).wait_send()
        for j, way in early_turns:
            early_reduce(way, step, j).wait_send()
            early_gather(way, step, j).wait_send()
        return 0

    def end_side(step, _):
        for j, way in early_turns:
            halve_copy(way, step, j).wait_send()
            join_copy(way, step, j, own_spots[way]).wait_send()
        return 0

    lax.fori_loop(0, chips - 1, end_ring, 0)
    lax.fori_loop(0, chips, end_side, 0)
    for j, way in late_turns:
        swap_copy(way, j).wait_send()


def deliver_kernel(*refs):
    count = len(refs) // 2
    for source, target in zip(refs[:count], refs[count:]):
        target[...] = source[...].reshape(target.shape)


def deliver(values):
    vmem = pl.BlockSpec(memory_space=pltpu.VMEM)
    return pl.pallas_call(
        deliver_kernel,
        out_shape=tuple(
            jax.ShapeDtypeStruct(v.shape[1:] if v.shape[0] == 1 else v.shape, v.dtype) for v in values
        ),
        in_specs=[vmem] * len(values),
        out_specs=(vmem,) * len(values),
        compiler_params=pltpu.CompilerParams(vmem_limit_bytes=60 << 20),
        name="deliver",
    )(*values)


def on_device(
    ssd_input,
    gate_input,
    state_maps,
    step_raw,
    step_bias,
    decay_rate,
    skip_gain,
    norm_gain,
    out_weight,
    reward_head,
    traj_lengths,
    step_pairs,
):
    tokens, channels = ssd_input.shape
    heads = step_raw.shape[1]
    model_width = out_weight.shape[0]
    seq_count, tensor_count = lax.axis_size("seq"), lax.axis_size("tensor")
    chips = tensor_count // 2
    late_width = model_width // (2 * chips)
    early_width = late_width // 2
    late_pieces, early_pieces = 1, 1
    piece = tokens * 10 // 24
    steps = chips - 1
    reach = -(-(longest - 1) // tokens)
    bf16, f32 = jnp.bfloat16, jnp.float32

    operands = (
        ssd_input,
        gate_input,
        state_maps.reshape(2 * tokens, STATE),
        step_raw.T,
        step_bias,
        decay_rate,
        skip_gain,
        norm_gain[None, :],
        out_weight,
        reward_head[None, :],
        traj_lengths[None, :],
        step_pairs[None, :],
    )
    vmem = pl.BlockSpec(memory_space=pltpu.VMEM)
    hbm = pl.BlockSpec(memory_space=pltpu.HBM)
    smem = pl.BlockSpec(memory_space=pltpu.SMEM)
    results = pl.pallas_call(
        layer_kernel,
        out_shape=(
            jax.ShapeDtypeStruct((1, tokens), f32),
            jax.ShapeDtypeStruct((tokens, channels), bf16),
            jax.ShapeDtypeStruct((tokens, channels), bf16),
            jax.ShapeDtypeStruct((2 * tokens, STATE), bf16),
            jax.ShapeDtypeStruct((heads, tokens), f32),
        ),
        in_specs=[hbm] * 4 + [smem] * 3 + [hbm] * 5,
        out_specs=(vmem,) * 5,
        scratch_shapes=[
            pltpu.VMEM((model_width, channels), bf16),
            pltpu.VMEM((tokens, channels), bf16),
            pltpu.VMEM((tokens, channels), bf16),
            pltpu.VMEM((2 * tokens, STATE), bf16),
            pltpu.VMEM((heads, tokens), f32),
            pltpu.VMEM((1, channels), f32),
            pltpu.VMEM((1, model_width), f32),
            pltpu.VMEM((1, traj_lengths.shape[0]), jnp.int32),
            pltpu.VMEM((1, step_pairs.shape[0]), jnp.int32),
            pltpu.VMEM((2 * tokens, STATE), f32),
            pltpu.VMEM((tokens, STATE), bf16),
            pltpu.VMEM((tokens, STATE), bf16),
            pltpu.VMEM((tokens, BLOCK), f32),
            pltpu.VMEM((heads, tokens, tokens), f32),
            pltpu.VMEM((tokens, tokens), f32),
            pltpu.VMEM((tokens, channels), f32),
            pltpu.VMEM((tokens, channels), f32),
            pltpu.VMEM((STATE, channels), f32),
            pltpu.VMEM((tokens, channels), bf16),
            pltpu.VMEM((tokens, channels), bf16),
            pltpu.VMEM((tokens, BLOCK), f32),
            pltpu.VMEM((tokens, BLOCK), f32),
            pltpu.VMEM((STATE + 16, channels), bf16),
            pltpu.VMEM((reach, STATE + 16, channels), bf16),
            pltpu.VMEM((STATE + 16, channels), bf16),
            pltpu.VMEM((reach, STATE + 16, channels), bf16),
            pltpu.VMEM((tokens, channels), bf16),
            pltpu.VMEM((tokens, channels), bf16),
            pltpu.VMEM((tokens, channels), f32),
            pltpu.VMEM((tokens, STATE), f32),
            pltpu.VMEM((tokens, BLOCK), f32),
            pltpu.VMEM((8, tokens), f32),
            pltpu.VMEM((tokens, channels), f32),
            pltpu.VMEM((seq_count, 8, tokens), f32),
            pltpu.VMEM((2, steps, late_pieces, piece, late_width), bf16),
            pltpu.VMEM((2, steps, late_pieces, piece, late_width), bf16),
            pltpu.VMEM((2, late_pieces, piece, late_width), bf16),
            pltpu.VMEM((2, late_pieces, piece, late_width), bf16),
            pltpu.VMEM((chips, 2, late_pieces, piece, late_width), bf16),
            pltpu.VMEM((2, steps, early_pieces, tokens - piece, early_width), bf16),
            pltpu.VMEM((2, steps, early_pieces, tokens - piece, early_width), bf16),
            pltpu.VMEM((2, chips, early_pieces, tokens - piece, early_width), bf16),
            pltpu.VMEM((2, chips, early_pieces, tokens - piece, early_width), bf16),
            pltpu.VMEM((chips, 2, 2, early_pieces, tokens - piece, early_width), bf16),
            pltpu.VMEM((8, tokens), f32),
            pltpu.VMEM((tensor_count, 8, tokens), f32),
            pltpu.VMEM((8, tokens), f32),
            pltpu.VMEM((STATE, channels), bf16),
            pltpu.VMEM((STATE, channels), bf16),
            pltpu.VMEM((STATE, channels), bf16),
            pltpu.VMEM((STATE, channels), bf16),
            pltpu.VMEM((STATE, channels), f32),
            pltpu.VMEM((tokens, channels), f32),
            pltpu.VMEM((tokens, BLOCK), f32),
            pltpu.VMEM((tokens, BLOCK), f32),
            pltpu.SemaphoreType.DMA((9,)),
            pltpu.SemaphoreType.DMA((2,)),
            pltpu.SemaphoreType.DMA((2,)),
            pltpu.SemaphoreType.DMA((reach,)),
            pltpu.SemaphoreType.DMA((reach,)),
            pltpu.SemaphoreType.DMA((reach,)),
            pltpu.SemaphoreType.DMA((reach,)),
            pltpu.SemaphoreType.DMA((2, steps, late_pieces)),
            pltpu.SemaphoreType.DMA((2, steps, late_pieces)),
            pltpu.SemaphoreType.DMA((2, late_pieces)),
            pltpu.SemaphoreType.DMA((2, late_pieces)),
            pltpu.SemaphoreType.DMA((2, steps, late_pieces)),
            pltpu.SemaphoreType.DMA((2, steps, late_pieces)),
            pltpu.SemaphoreType.DMA((2, steps, early_pieces)),
            pltpu.SemaphoreType.DMA((2, steps, early_pieces)),
            pltpu.SemaphoreType.DMA((2, steps, early_pieces)),
            pltpu.SemaphoreType.DMA((2, steps, early_pieces)),
            pltpu.SemaphoreType.DMA((2, chips, early_pieces)),
            pltpu.SemaphoreType.DMA((2, chips, early_pieces)),
            pltpu.SemaphoreType.DMA((2, chips, early_pieces)),
            pltpu.SemaphoreType.DMA((2, chips, early_pieces)),
            pltpu.SemaphoreType.DMA((tensor_count,)),
            pltpu.SemaphoreType.DMA((tensor_count,)),
            pltpu.SemaphoreType.DMA((seq_count,)),
            pltpu.SemaphoreType.DMA((seq_count,)),
        ],
        compiler_params=pltpu.CompilerParams(
            collective_id=0, has_side_effects=True, vmem_limit_bytes=60 << 20
        ),
        name="layer",
    )(*operands)
    rewards, dx, dz, dmaps, dstep = deliver(results)
    return (
        rewards,
        dx,
        dz,
        dmaps.reshape(tokens, 2, STATE),
        dstep.T,
    )


def solution(mesh):
    return jax.shard_map(
        on_device,
        mesh=mesh,
        in_specs=(
            P("seq", "tensor"),
            P("seq", "tensor"),
            P("seq", None, "tensor"),
            P("seq", "tensor"),
            P("tensor"),
            P("tensor"),
            P("tensor"),
            P("tensor"),
            P(None, "tensor"),
            P(),
            P(),
            P(),
        ),
        out_specs=(
            P("seq"),
            P("seq", "tensor"),
            P("seq", "tensor"),
            P("seq", None, "tensor"),
            P("seq", "tensor"),
        ),
        check_vma=False,
    )
```
